128 devices in a mesh: dp: 8 (over x_hi, z), cent: 16 (over x_lo, y, core).
Axes of the slice: x: 4 (x_hi: 2, x_lo: 2; x = x_hi * 2 + x_lo), y: 4, z: 4, core: 2. Of those that a mesh axis runs over, the one named last changes fastest.
Arguments:
- points: bfloat16 [16384, 1024], P(('dp', 'cent')), may hold values from -6 to 6
- centroids: bfloat16 [32768, 1024], P('cent'), may hold values from -6 to 6
Outputs:
- centroids_next: float32 [1024, 32768], P('dp', 'cent')
The draws below stay inside these ranges and needn't reach their ends.
All inputs are finite; a program needn't handle non-finite values.
Results may differ from the reference program's by a relative error of at most 0.007.
Values may be sent and summed in bfloat16 or wider, within the bound.
No kernel may reach another device: no remote copies, remote signals or barrier semaphores. Data moves between devices by JAX's collectives and lax.ppermute only.
A program may use at most 128 MiB of HBM per device.

```python
import jax
import jax.numpy as jnp
from jax import lax

D = 1024
K = 32768
ROWS = 16384
N_DP = 8


def centroid_rows(key, row_ids):
    base_key = jax.random.fold_in(key, 9137)

    def single_row(row_id):
        row_key = jax.random.fold_in(base_key, row_id)
        return jnp.clip(jax.random.normal(row_key, (D,), jnp.float32), -6.0, 6.0)
    return jax.vmap(single_row)(row_ids)


def draw_centroids(key, part):
    matrix = centroid_rows(key, jnp.arange(K, dtype=jnp.int32))
    return matrix.astype(jnp.bfloat16)


def draw_points(key, part):
    value_key = jax.random.fold_in(key, 4421)
    return jnp.clip(jax.random.normal(value_key, (ROWS, D), jnp.float32), -6.0, 6.0).astype(jnp.bfloat16)


def setup_inputs(seed: int = 0) -> dict:
    keys = jax.random.split(jax.random.key(seed), 3)
    points = draw_points(jax.random.fold_in(keys[2], 71), 0)
    centroids = draw_centroids(jax.random.fold_in(keys[2], 71), 0)
    return dict(points=points, centroids=centroids)


BETA_GAIN = 4.0
PRIOR = 0.5


def reference(points, centroids):
    sharpness = BETA_GAIN * D ** -0.5
    cent_vals = centroids.astype(jnp.float32)
    sqnorm = jnp.sum(cent_vals * cent_vals, axis=1)
    group_size = ROWS // N_DP
    block_rows = min(512, group_size)
    grouped = points.reshape(N_DP, group_size // block_rows, block_rows, D)

    def block_step(carry, xblock):
        counts_acc, numer_acc = carry
        point_vals = xblock.astype(jnp.float32)
        dots = jnp.dot(point_vals, cent_vals.T, precision=lax.Precision.HIGHEST)
        logits = sharpness * (dots - 0.5 * sqnorm[None, :])
        row_top = jnp.max(logits, axis=1, keepdims=True)
        weights = jnp.exp(logits - row_top)
        row_total = jnp.sum(weights, axis=1, keepdims=True)
        resp = lax.optimization_barrier((weights / row_total).astype(jnp.bfloat16)).astype(jnp.float32)
        counts_acc = counts_acc + jnp.sum(resp, axis=0)
        numer_acc = numer_acc + jnp.dot(resp.T, point_vals, precision=lax.Precision.HIGHEST)
        return (counts_acc, numer_acc), None

    def group_step(carry, blocks):
        counts_all, numer_all = carry
        begin = (jnp.zeros((K,), jnp.float32), jnp.zeros((K, D), jnp.float32))
        (counts_part, numer_part), _ = lax.scan(block_step, begin, blocks)
        numer_part = lax.optimization_barrier(numer_part.astype(jnp.bfloat16)).astype(jnp.float32)
        return (counts_all + counts_part, numer_all + numer_part), None

    begin_all = (jnp.zeros((K,), jnp.float32), jnp.zeros((K, D), jnp.float32))
    (counts, numer), _ = lax.scan(group_step, begin_all, grouped)
    updated = (numer + PRIOR * cent_vals) / (counts[:, None] + PRIOR)
    return updated.T
```

```python
import functools
import math

import jax
import jax.numpy as jnp
from jax import lax
from jax.experimental import pallas as pl
from jax.experimental.pallas import tpu as pltpu
from jax.sharding import PartitionSpec as P

BETA_GAIN = 4.0
PRIOR = 0.5
F32 = jnp.float32
BF16 = jnp.bfloat16

NX, NY, NZ = 4, 4, 4
AXES = ("dp", "cent")
COUNT_ROWS = 32
GROUPS = ((2, 1), (3, 0))


def _send(a, move):
    pairs = []
    for xh in range(2):
        for z in range(NZ):
            for xl in range(2):
                for y in range(NY):
                    for core in range(2):
                        src = (xh * 4 + z) * 16 + (xl * 4 + y) * 2 + core
                        x2, y2, z2, core2 = move(xh * 2 + xl, y, z, core)
                        x2, y2, z2 = x2 % NX, y2 % NY, z2 % NZ
                        dst = ((x2 // 2) * 4 + z2) * 16 + ((x2 % 2) * 4 + y2) * 2 + core2
                        pairs.append((src, dst))
    return lax.ppermute(a, AXES, pairs)


def send_first(a, d):
    return _send(a, lambda x, y, z, c: (x, y + d, z, c) if c == 0 else (x + d, y, z, c))


def send_second(a, d):
    return _send(a, lambda x, y, z, c: (x + d, y, z, c) if c == 0 else (x, y + d, z, c))


def send_core(a):
    return _send(a, lambda x, y, z, c: (x, y, z, 1 - c))


def send_owner(a, dxh, dz):
    return _send(a, lambda x, y, z, c: (x + 2 * dxh, y, z + dz, c))


def _full(shape):
    return pl.BlockSpec(shape, lambda *_: (0,) * len(shape))


def _norm_kernel(a_ref, b_ref, o_ref):
    for i, r in enumerate((a_ref, b_ref)):
        v = r[...].astype(F32)
        s = 0.5 * jnp.sum(v * v, axis=1, keepdims=True)
        o_ref[i] = jnp.broadcast_to(s, (s.shape[0], 128))


def half_norms(own, sib):
    k, d = own.shape
    step = 256
    return pl.pallas_call(
        _norm_kernel,
        out_shape=jax.ShapeDtypeStruct((2, k, 128), F32),
        grid=(k // step,),
        in_specs=[pl.BlockSpec((step, d), lambda i: (i, 0))] * 2,
        out_specs=pl.BlockSpec((2, step, 128), lambda i: (0, i, 0)),
        name="half_norms",
    )(own, sib)


def _score_kernel(gain, x_ref, own_ref, sib_ref, h_ref, w_ref, st_ref, u_ref):
    x = x_ref[...]
    rb = x.shape[0]
    k = own_ref.shape[0]
    kb = 256
    maxima = []
    for b, c_ref in enumerate((own_ref, sib_ref)):
        m = None
        for j in range(k // kb):
            rows = slice(j * kb, (j + 1) * kb)
            dots = lax.dot_general(
                c_ref[rows, :], x, (((1,), (1,)), ((), ())), preferred_element_type=F32
            )
            u = dots - jnp.tile(h_ref[b, rows, :], (1, rb // 128))
            u_ref[b, rows, :] = u
            mj = jnp.max(u, axis=0, keepdims=True)
            m = mj if m is None else jnp.maximum(m, mj)
        maxima.append(m)
    for b in range(2):
        m = maxima[b]
        s = None
        for j in range(k // kb):
            rows = slice(j * kb, (j + 1) * kb)
            w = jnp.exp2((u_ref[b, rows, :] - m) * gain)
            sj = jnp.sum(w, axis=0, keepdims=True)
            s = sj if s is None else s + sj
            w_ref[b, rows, :] = w.astype(BF16)
        st_ref[2 * b : 2 * b + 1, :] = m
        st_ref[2 * b + 1 : 2 * b + 2, :] = s
    st_ref[4:8, :] = jnp.zeros((4, rb), F32)


def score(x, own, sib, h, gain):
    r, d = x.shape
    k = own.shape[0]
    rb = min(256, r)
    return pl.pallas_call(
        functools.partial(_score_kernel, gain),
        out_shape=(
            jax.ShapeDtypeStruct((2, k, r), BF16),
            jax.ShapeDtypeStruct((8, r), F32),
        ),
        grid=(r // rb,),
        in_specs=[
            pl.BlockSpec((rb, d), lambda i: (i, 0)),
            _full((k, d)),
            _full((k, d)),
            _full((2, k, 128)),
        ],
        out_specs=(
            pl.BlockSpec((2, k, rb), lambda i: (0, 0, i)),
            pl.BlockSpec((8, rb), lambda i: (0, i)),
        ),
        scratch_shapes=[pltpu.VMEM((2, k, rb), F32)],
        compiler_params=pltpu.CompilerParams(vmem_limit_bytes=40 << 20),
        cost_estimate=pl.CostEstimate(
            flops=4 * r * k * d, bytes_accessed=4 * k * d + 2 * r * d + 4 * r * k,
            transcendentals=2 * r * k,
        ),
        name="score",
    )(x, own, sib, h)


def _sum_kernel(half, n_arr, n_blk, stacked, has_add, fb_ref, *refs):
    w_refs = refs[:n_arr]
    x_refs = refs[n_arr : n_arr + n_arr * n_blk]
    pos = n_arr + n_arr * n_blk
    sc_ref = refs[pos]
    pos += 1
    add_ref = None
    if has_add:
        add_ref = refs[pos]
        pos += 1
    n_out = 1 if stacked else n_blk
    outs = refs[pos : pos + n_out]
    xb_ref, cnt_ref = refs[pos + n_out :]
    i = pl.program_id(0)
    steps = pl.num_programs(0)
    kb = w_refs[0].shape[1]
    r = w_refs[0].shape[2]
    k = outs[0].shape[-2] - COUNT_ROWS

    @pl.when(i == 0)
    def _():
        for a in range(n_arr):
            for f in range(n_blk):
                xb_ref[a * r : (a + 1) * r, f * 128 : (f + 1) * 128] = x_refs[a * n_blk + f][...]

    acc = None
    lanes = None
    for a in range(n_arr):
        sc = sc_ref[half : half + 1, a * r : (a + 1) * r]
        w = (w_refs[a][0].astype(F32) * sc).astype(BF16)
        wf = w.astype(F32)
        for t in range(r // 128):
            part = wf[:, t * 128 : (t + 1) * 128]
            lanes = part if lanes is None else lanes + part
        d = jnp.dot(w, xb_ref[a * r : (a + 1) * r, :], preferred_element_type=F32)
        acc = d if acc is None else acc + d
    col = jnp.sum(lanes.T, axis=0, keepdims=True)
    per = kb // 128
    rows = jnp.concatenate([col[:, t * 128 : (t + 1) * 128] for t in range(per)], axis=0)
    for j in range(k // kb):

        @pl.when(i == j)
        def _():
            cnt_ref[j * per : (j + 1) * per, :] = rows

    row0 = pl.multiple_of(i * kb, kb)
    for f in range(n_blk):
        v = acc[:, f * 128 : (f + 1) * 128]
        if has_add:
            v = v + add_ref[f, pl.ds(row0, kb), :].astype(F32)
        v = v.astype(BF16)
        if stacked:
            outs[0][f, pl.ds(row0, kb), :] = v
        else:
            outs[f][pl.ds(row0, kb), :] = v

    @pl.when(i == steps - 1)
    def _():
        c = cnt_ref[...]
        if has_add:
            t = add_ref[0, k : k + COUNT_ROWS, :].astype(F32)
            c = c + ((t[0:8] + t[8:16]) + t[16:24])
        hi = c.astype(BF16).astype(F32)
        mid = (c - hi).astype(BF16).astype(F32)
        lo = (c - hi) - mid
        packed = jnp.concatenate([hi, mid, lo, jnp.zeros_like(lo)], axis=0).astype(BF16)
        for f in range(n_blk):
            if stacked:
                outs[0][f, k : k + COUNT_ROWS, :] = packed
            else:
                outs[f][k : k + COUNT_ROWS, :] = packed


def weighted_sums(half, ws, xs, scales, blocks, add=None, stacked=False):
    n_arr, n_blk = len(ws), blocks.shape[0]
    k, r = ws[0].shape[1:]
    kb = 256
    rows = k + COUNT_ROWS
    in_specs = [pl.BlockSpec((1, kb, r), lambda i, fb: (half, i, 0)) for _ in ws]
    for _ in xs:
        for f in range(n_blk):
            in_specs.append(pl.BlockSpec((r, 128), lambda i, fb, f=f: (0, fb[f])))
    in_specs.append(_full(scales.shape))
    operands = list(ws)
    for x in xs:
        operands += [x] * n_blk
    operands.append(scales)
    if add is not None:
        in_specs.append(_full(add.shape))
        operands.append(add)
    if stacked:
        out_shape = [jax.ShapeDtypeStruct((n_blk, rows, 128), BF16)]
        out_specs = [_full((n_blk, rows, 128))]
    else:
        out_shape = [jax.ShapeDtypeStruct((rows, 128), BF16)] * n_blk
        out_specs = [_full((rows, 128))] * n_blk
    return pl.pallas_call(
        functools.partial(_sum_kernel, half, n_arr, n_blk, stacked, add is not None),
        out_shape=out_shape,
        grid_spec=pltpu.PrefetchScalarGridSpec(
            num_scalar_prefetch=1,
            grid=(k // kb,),
            in_specs=in_specs,
            out_specs=out_specs,
            scratch_shapes=[
                pltpu.VMEM((n_arr * r, n_blk * 128), BF16),
                pltpu.VMEM((8, 128), F32),
            ],
        ),
        compiler_params=pltpu.CompilerParams(vmem_limit_bytes=40 << 20),
        cost_estimate=pl.CostEstimate(
            flops=2 * k * n_arr * r * n_blk * 128,
            bytes_accessed=2 * n_arr * r * (k + n_blk * 128),
            transcendentals=0,
        ),
        name="sums_sib" if add is None else "sums_own",
    )(blocks, *operands)


def _final_kernel(n, idx_ref, *refs):
    parts = (refs[:n], refs[n : 2 * n])
    c_ref, o_ref = refs[2 * n :]
    k = c_ref.shape[0] // 2
    for j in range(2):
        side = idx_ref[0] if j == 0 else 1 - idx_ref[0]
        off = pl.multiple_of(side * k, k)
        total = None
        for p in parts[j]:
            v = p[...].astype(F32)
            total = v if total is None else total + v
        t = total[k : k + 24]
        c = (t[0:8] + t[8:16]) + t[16:24]
        cnt = jnp.concatenate([c[q : q + 1, :] for q in range(k // 128)], axis=1)
        top = total[:k] + PRIOR * c_ref[pl.ds(off, k), :].astype(F32)
        o_ref[:, pl.ds(off, k)] = top.T / (cnt + PRIOR)


def finish(idx, mine, other, centroids):
    rows = mine[0].shape[0]
    k2 = centroids.shape[0]
    return pl.pallas_call(
        functools.partial(_final_kernel, len(mine)),
        out_shape=jax.ShapeDtypeStruct((128, k2), F32),
        grid_spec=pltpu.PrefetchScalarGridSpec(
            num_scalar_prefetch=1,
            grid=(1,),
            in_specs=[_full((rows, 128))] * (2 * len(mine))
            + [pl.BlockSpec((k2, 128), lambda i, idx: (0, idx[1]))],
            out_specs=_full((128, k2)),
        ),
        compiler_params=pltpu.CompilerParams(vmem_limit_bytes=40 << 20),
        name="finish",
    )(idx, *mine, *other, centroids)


def _merge(pairs, gain):
    m = functools.reduce(jnp.maximum, [p[0] for p in pairs])
    s = sum(p[1] * jnp.exp2((p[0] - m) * gain) for p in pairs)
    return m, s


def local(points, centroids):
    features = points.shape[1]
    gain = BETA_GAIN * features ** (-0.5) * math.log2(math.e)
    dp = lax.axis_index("dp")
    xh, z = dp // NZ, dp % NZ
    half_cents = centroids.shape[0] // 2

    got = [points] + [send_first(points, d) for d in (1, 2, 3)]
    own = lax.dynamic_slice_in_dim(centroids, xh * half_cents, half_cents, 0)
    sib = send_core(own)
    line = jnp.concatenate(got, axis=0)
    xs = [line] + [send_second(line, d) for d in (1, 2, 3)]
    h = half_norms(own, sib)

    ws, stats = [None] * 4, [None] * 4
    for k in (0, 1, 3, 2):
        ws[k], stats[k] = score(xs[k], own, sib, h, gain)
    st = jnp.stack(stats)
    mb, sb = st[:, 0:4:2, :], st[:, 1:4:2, :]
    m, s = _merge([(mb[:, b], sb[:, b]) for b in range(2)], gain)
    pack = jnp.stack([m, s]).reshape(2, 4, 4, -1)
    every = [pack] + [jnp.roll(send_first(pack, d), d, axis=2) for d in (1, 2, 3)]
    pack = jnp.stack(_merge([(e[0], e[1]) for e in every], gain))
    every = [pack] + [jnp.roll(send_second(pack, d), d, axis=1) for d in (1, 2, 3)]
    top, total = _merge([(e[0], e[1]) for e in every], gain)
    top, total = top.reshape(4, 1, -1), total.reshape(4, 1, -1)
    scales = jnp.exp2((mb - top) * gain) / total
    scales = scales.transpose(1, 0, 2).reshape(2, -1)

    mine, other = [], []
    for group in GROUPS:
        blocks = jnp.stack(
            [((xh + dxh) % 2) * NZ + (z + dz) % NZ for dz in group for dxh in (1, 0)]
        ).astype(jnp.int32)
        (part,) = weighted_sums(1, ws, xs, scales, blocks, stacked=True)
        part = send_core(part)
        sums = weighted_sums(0, ws, xs, scales, blocks, add=part)
        for n, (dz, dxh) in enumerate((dz, dxh) for dz in group for dxh in (1, 0)):
            if dxh == 0:
                mine.append(sums[n] if dz == 0 else send_owner(sums[n], 0, dz))
            else:
                other.append(send_owner(sums[n], 1, dz))
    idx = jnp.stack([xh, dp]).astype(jnp.int32)
    return finish(idx, mine, other, centroids)


def solution(mesh):
    return jax.shard_map(
        local,
        mesh=mesh,
        in_specs=(P(("dp", "cent"), None), P("cent", None)),
        out_specs=P("dp", "cent"),
        check_vma=False,
    )
```

```python
import functools
import math

import jax
import jax.numpy as jnp
from jax import lax
from jax.experimental import pallas as pl
from jax.experimental.pallas import tpu as pltpu
from jax.sharding import PartitionSpec as P

BETA_GAIN = 4.0
PRIOR = 0.5
F32 = jnp.float32
BF16 = jnp.bfloat16

NX, NY, NZ = 4, 4, 4
AXES = ("dp", "cent")
COUNT_ROWS = 32
SHIFTS = (2, 1, 3, 0)
VMEM = pl.BlockSpec(memory_space=pltpu.VMEM)
SMEM = pl.BlockSpec(memory_space=pltpu.SMEM)


def _send(a, move):
    pairs = []
    for xh in range(2):
        for z in range(NZ):
            for xl in range(2):
                for y in range(NY):
                    for core in range(2):
                        src = (xh * 4 + z) * 16 + (xl * 4 + y) * 2 + core
                        x2, y2, z2, core2 = move(xh * 2 + xl, y, z, core)
                        x2, y2, z2 = x2 % NX, y2 % NY, z2 % NZ
                        dst = ((x2 // 2) * 4 + z2) * 16 + ((x2 % 2) * 4 + y2) * 2 + core2
                        pairs.append((src, dst))
    return lax.ppermute(a, AXES, pairs)


def send_first(a, d):
    return _send(a, lambda x, y, z, c: (x, y + d, z, c) if c == 0 else (x + d, y, z, c))


def send_second(a, d):
    return _send(a, lambda x, y, z, c: (x + d, y, z, c) if c == 0 else (x, y + d, z, c))


def send_core(a):
    return _send(a, lambda x, y, z, c: (x, y, z, 1 - c))


def send_z(a, d):
    return _send(a, lambda x, y, z, c: (x, y, z + d, c))


def send_far(a):
    return _send(a, lambda x, y, z, c: (x + 2, y, z, c))


def _params(mib):
    return pltpu.CompilerParams(vmem_limit_bytes=mib << 20)


def _norm_kernel(idx_ref, c_ref, o_ref):
    k = o_ref.shape[0]
    step = 128
    for j in range(k // step):
        v = c_ref[pl.ds(pl.multiple_of(idx_ref[0] * k + j * step, step), step), :].astype(F32)
        s = 0.5 * jnp.sum(v * v, axis=1, keepdims=True)
        o_ref[j * step : (j + 1) * step, :] = jnp.broadcast_to(s, (step, 128))


def half_norms(idx, cents):
    k, d = cents.shape
    return pl.pallas_call(
        _norm_kernel,
        out_shape=jax.ShapeDtypeStruct((k // 2, 128), F32),
        in_specs=[SMEM, VMEM],
        out_specs=VMEM,
        compiler_params=_params(8),
        cost_estimate=pl.CostEstimate(
            flops=k * d, bytes_accessed=k * d * 2, transcendentals=0
        ),
        name="half_norms",
    )(idx, cents)


def _score_kernel(gain, n_x, idx_ref, *refs):
    x_refs = refs[:n_x]
    c_refs, h_refs = refs[n_x : n_x + 2], refs[n_x + 2 : n_x + 4]
    w_ref, st_ref, xp_ref, u_ref, xt_ref = refs[-5:]
    k = h_refs[0].shape[0]
    r = w_ref.shape[2]
    kb = 256
    base = idx_ref[0] * k
    pos = 0
    for x_ref in x_refs:
        n = x_ref.shape[0]
        xt_ref[:, pos : pos + n] = x_ref[...].T
        pos += n

    def dots(b, j):
        rows = slice(j * kb, (j + 1) * kb)
        c = c_refs[b][pl.ds(pl.multiple_of(base + j * kb, kb), kb), :]
        u = jnp.dot(c, xt_ref[...], preferred_element_type=F32)
        u = u - jnp.tile(h_refs[b][rows, :], (1, r // 128))
        u_ref[b, rows, :] = u
        return jnp.max(u, axis=0, keepdims=True)

    def weights(b, j, m):
        rows = slice(j * kb, (j + 1) * kb)
        w = jnp.exp2((u_ref[b, rows, :] - m) * gain)
        w_ref[b, rows, :] = w.astype(BF16)
        return jnp.sum(w, axis=0, keepdims=True)

    def largest(ms):
        return functools.reduce(jnp.maximum, ms)

    nj = k // kb
    m0 = largest([dots(0, j) for j in range(nj)])
    ms, ss = [], []
    for j in range(nj):
        ms.append(dots(1, j))
        ss.append(weights(0, j, m0))
    m1 = largest(ms)
    st_ref[0:1, :] = m0
    st_ref[1:2, :] = sum(ss)
    for f in range(2 * NZ):
        off = pl.multiple_of(idx_ref[2 + f] * 128, 128)
        pos = 0
        for x_ref in x_refs:
            n = x_ref.shape[0]
            xp_ref[pos : pos + n, f * 128 : (f + 1) * 128] = x_ref[:, pl.ds(off, 128)]
            pos += n
    st_ref[2:3, :] = m1
    st_ref[3:4, :] = sum([weights(1, j, m1) for j in range(nj)])
    st_ref[4:8, :] = jnp.zeros((4, r), F32)


def score(idx, xs, cents, norms, gain, after):
    r, d = sum(x.shape[0] for x in xs), xs[0].shape[1]
    k = norms[0].shape[0]
    return pl.pallas_call(
        functools.partial(_score_kernel, gain, len(xs)),
        out_shape=(
            jax.ShapeDtypeStruct((2, k, r), BF16),
            jax.ShapeDtypeStruct((8, r), F32),
            jax.ShapeDtypeStruct((r, d), BF16),
        ),
        in_specs=[SMEM] + [VMEM] * (len(xs) + 4 + len(after)),
        out_specs=(VMEM, VMEM, VMEM),
        scratch_shapes=[pltpu.VMEM((2, k, r), F32), pltpu.VMEM((d, r), BF16)],
        compiler_params=_params(14),
        cost_estimate=pl.CostEstimate(
            flops=8 * r * k * d, bytes_accessed=2 * r * d, transcendentals=2 * r * k
        ),
        name="score",
    )(idx, *xs, *cents, *norms, *after)


def _sum_kernel(half, group, n_arr, has_add, *refs):
    w_refs, x_refs, sc_refs = refs[:n_arr], refs[n_arr : 2 * n_arr], refs[2 * n_arr]
    pos = 2 * n_arr + 1
    add_ref = refs[pos] if has_add else None
    outs = refs[pos + 1 if has_add else pos : -1]
    cnt_ref = refs[-1]
    k, r = w_refs[0].shape[1:]
    kb = 256
    per = kb // 128
    n_blk = NZ
    cols = slice(group * n_blk * 128, (group + 1) * n_blk * 128)

    def put(f, rows, v):
        if has_add:
            outs[f][rows, :] = v
        else:
            outs[0][f, rows, :] = v

    for j in range(k // kb):
        rows = slice(j * kb, (j + 1) * kb)
        acc, lanes = None, None
        for a in range(n_arr):
            sc = sc_refs[half : half + 1, a * r : (a + 1) * r]
            w = (w_refs[a][half, rows, :].astype(F32) * sc).astype(BF16)
            wf = w.astype(F32)
            for t in range(r // 128):
                part = wf[:, t * 128 : (t + 1) * 128]
                lanes = part if lanes is None else lanes + part
            d = jnp.dot(w, x_refs[a][:, cols], preferred_element_type=F32)
            acc = d if acc is None else acc + d
        col = jnp.sum(lanes.T, axis=0, keepdims=True)
        for t in range(per):
            cnt_ref[j * per + t : j * per + t + 1, :] = col[:, t * 128 : (t + 1) * 128]
        for f in range(n_blk):
            v = acc[:, f * 128 : (f + 1) * 128]
            if has_add:
                v = v + add_ref[f, rows, :].astype(F32)
            put(f, rows, v.astype(BF16))
    c = cnt_ref[...]
    if has_add:
        c = c + _unpack_counts(add_ref[0, k : k + COUNT_ROWS, :])
    packed = _pack_counts(c)
    for f in range(n_blk):
        put(f, slice(k, k + COUNT_ROWS), packed)


def _pack_counts(c):
    hi = c.astype(BF16).astype(F32)
    mid = (c - hi).astype(BF16).astype(F32)
    lo = (c - hi) - mid
    return jnp.concatenate([hi, mid, lo, jnp.zeros_like(lo)], axis=0).astype(BF16)


def _unpack_counts(rows):
    t = rows.astype(F32)
    return (t[0:8] + t[8:16]) + t[16:24]


def weighted_sums(half, group, ws, xs, scales, add=None):
    n_arr = len(ws)
    k, r = ws[0].shape[1:]
    rows = k + COUNT_ROWS
    operands = [*ws, *xs, scales]
    if add is None:
        out_shape = [jax.ShapeDtypeStruct((NZ, rows, 128), BF16)]
    else:
        operands.append(add)
        out_shape = [jax.ShapeDtypeStruct((rows, 128), BF16)] * NZ
    return pl.pallas_call(
        functools.partial(_sum_kernel, half, group, n_arr, add is not None),
        out_shape=out_shape,
        in_specs=[VMEM] * len(operands),
        out_specs=[VMEM] * len(out_shape),
        scratch_shapes=[pltpu.VMEM((8, 128), F32)],
        compiler_params=_params(14),
        cost_estimate=pl.CostEstimate(
            flops=4 * k * n_arr * r * NZ * 128, bytes_accessed=2 * rows * NZ * 128,
            transcendentals=0,
        ),
        name="sums_sib" if add is None else "sums_own",
    )(*operands)


def _total(parts):
    total = None
    for p in parts:
        v = p[...].astype(F32)
        total = v if total is None else total + v
    return total


def _add_kernel(*refs):
    o_ref = refs[-1]
    k = o_ref.shape[0] - COUNT_ROWS
    total = _total(refs[:-1])
    o_ref[:k, :] = total[:k].astype(BF16)
    o_ref[k:, :] = _pack_counts(_unpack_counts(total[k:]))


def add_blocks(parts):
    return pl.pallas_call(
        _add_kernel,
        out_shape=jax.ShapeDtypeStruct(parts[0].shape, BF16),
        in_specs=[VMEM] * len(parts),
        out_specs=VMEM,
        compiler_params=_params(8),
        cost_estimate=pl.CostEstimate(
            flops=0, bytes_accessed=10 * parts[0].size, transcendentals=0
        ),
        name="add_blocks",
    )(*parts)


def _final_kernel(n, idx_ref, *refs):
    parts = (refs[:n], refs[n : n + 1])
    c_ref, o_ref = refs[n + 1 :]
    k = c_ref.shape[0] // 2
    for j in range(2):
        side = idx_ref[0] if j == 0 else 1 - idx_ref[0]
        off = pl.multiple_of(side * k, k)
        total = _total(parts[j])
        c = _unpack_counts(total[k:])
        cnt = jnp.concatenate([c[q : q + 1, :] for q in range(k // 128)], axis=1)
        cols = pl.ds(pl.multiple_of(idx_ref[1] * 128, 128), 128)
        top = total[:k] + PRIOR * c_ref[pl.ds(off, k), cols].astype(F32)
        o_ref[:, pl.ds(off, k)] = top.T / (cnt + PRIOR)


def finish(idx, mine, other, centroids):
    return pl.pallas_call(
        functools.partial(_final_kernel, len(mine)),
        out_shape=jax.ShapeDtypeStruct((128, centroids.shape[0]), F32),
        in_specs=[SMEM] + [VMEM] * (len(mine) + 2),
        out_specs=VMEM,
        compiler_params=_params(12),
        name="finish",
    )(idx, *mine, other, centroids)


def _slots():
    place = {}
    for a in range(4):
        place[0, a] = (0, a * 128)
        place[2, a] = (3, a * 128)
        place[1, a] = (1 if a < 2 else 2, (a % 2) * 128)
        place[3, a] = (1 if a >= 2 else 2, 256 + (a % 2) * 128)
    return [place[b, a] for b in range(4) for a in range(4)]


def _gather_slots(refs, row):
    return jnp.concatenate(
        [refs[n][row : row + 1, off : off + 128] for n, off in _slots()], axis=0
    )


def _merge(pairs, gain):
    m = functools.reduce(jnp.maximum, [p[0] for p in pairs])
    s = sum(p[1] * jnp.exp2((p[0] - m) * gain) for p in pairs)
    return m, s


def _shifted(v, d, axis):
    if d == 0:
        return v
    if axis == 1:
        return jnp.concatenate([v[16 - 4 * d :], v[: 16 - 4 * d]], axis=0)
    parts = []
    for b in range(0, 16, 4):
        parts += [v[b + 4 - d : b + 4], v[b : b + 4 - d]]
    return jnp.concatenate(parts, axis=0)


def _pack_kernel(gain, *refs):
    o_ref = refs[-1]
    pairs = [(_gather_slots(refs, 2 * b), _gather_slots(refs, 2 * b + 1)) for b in range(2)]
    o_ref[0], o_ref[1] = _merge(pairs, gain)


def _merge_kernel(gain, axis, *refs):
    o_ref = refs[-1]
    pairs = [
        (_shifted(refs[d][0], d, axis), _shifted(refs[d][1], d, axis)) for d in range(4)
    ]
    o_ref[0], o_ref[1] = _merge(pairs, gain)


def _scale_kernel(gain, axis, *refs):
    stats, o_ref = refs[4:8], refs[-1]
    pairs = [
        (_shifted(refs[d][0], d, axis), _shifted(refs[d][1], d, axis)) for d in range(4)
    ]
    top, total = _merge(pairs, gain)
    r = stats[0].shape[1]
    for b in range(2):
        q = jnp.exp2((_gather_slots(stats, 2 * b) - top) * gain) / total
        for i, (n, off) in enumerate(_slots()):
            o_ref[b : b + 1, n * r + off : n * r + off + 128] = q[i : i + 1, :]


def _small(kernel, shape, args, name):
    return pl.pallas_call(
        kernel,
        out_shape=jax.ShapeDtypeStruct(shape, F32),
        in_specs=[VMEM] * len(args),
        out_specs=VMEM,
        compiler_params=_params(2),
        name=name,
    )(*args)


def local(points, centroids):
    features = points.shape[1]
    gain = BETA_GAIN * features ** (-0.5) * math.log2(math.e)
    dp = lax.axis_index("dp")
    xh, z = dp // NZ, dp % NZ
    blocks = [(1 - xh) * NZ + (z + d) % NZ for d in SHIFTS]
    blocks += [xh * NZ + (z + d) % NZ for d in SHIFTS]
    idx = jnp.stack([xh, dp] + blocks).astype(jnp.int32)

    shards = [points] + [send_first(points, d) for d in (1, 2, 3)]
    cents = (centroids, send_core(centroids))
    line = jnp.concatenate(shards, axis=0)
    half = line.shape[0] // 2
    line_a, line_b = line[:half], line[half:]
    up_a, down_b = send_second(line_a, 1), send_second(line_b, 3)
    norms = [half_norms(idx, c) for c in cents]
    line_a, line_b, norms[1] = lax.optimization_barrier((line_a, line_b, norms[1]))
    up_b, down_a = send_second(line_b, 1), send_second(line_a, 3)

    ws, stats, xs = [], [], []

    def run(*xin):
        w, st, xp = score(idx, xin, cents, norms, gain, stats[-1:])
        ws.append(w)
        stats.append(st)
        xs.append(xp)

    run(line)
    up_a, down_b, stats[0] = lax.optimization_barrier((up_a, down_b, stats[0]))
    far_a, far_b = send_second(up_a, 1), send_second(down_b, 3)
    run(up_a, down_b)
    run(up_b, down_a)
    run(far_a, far_b)

    shape = (2, 16, 128)
    pack = _small(functools.partial(_pack_kernel, gain), shape, stats, "stats_pack")
    every = [pack] + [send_first(pack, d) for d in (1, 2, 3)]
    pack = _small(functools.partial(_merge_kernel, gain, 0), shape, every, "stats_merge")
    every = [pack] + [send_second(pack, d) for d in (1, 2, 3)]
    scales = _small(
        functools.partial(_scale_kernel, gain, 1),
        (8, sum(st.shape[1] for st in stats)),
        every + stats,
        "stats_scale",
    )

    swapped = [send_core(weighted_sums(1, g, ws, xs, scales)[0]) for g in range(2)]
    got = []
    for g in range(2):
        sums = weighted_sums(0, g, ws, xs, scales, add=swapped[g])
        got.append([sums[3]] + [send_z(sums[n], d) for n, d in enumerate(SHIFTS[:3])])
    other = send_far(add_blocks(got[0]))
    return finish(idx, got[1], other, centroids)


def solution(mesh):
    return jax.shard_map(
        local,
        mesh=mesh,
        in_specs=(P(("dp", "cent"), None), P("cent", None)),
        out_specs=P("dp", "cent"),
        check_vma=False,
    )
```

```python
import functools
import math

import jax
import jax.numpy as jnp
from jax import lax
from jax.experimental import pallas as pl
from jax.experimental.pallas import tpu as pltpu
from jax.sharding import PartitionSpec as P

BETA_GAIN = 4.0
PRIOR = 0.5
F32 = jnp.float32
BF16 = jnp.bfloat16

NX, NY, NZ = 4, 4, 4
AXES = ("dp", "cent")
COUNT_ROWS = 32
SHIFTS = (2, 1, 3, 0)
VMEM = pl.BlockSpec(memory_space=pltpu.VMEM)
SMEM = pl.BlockSpec(memory_space=pltpu.SMEM)


def _send(a, move):
    pairs = []
    for xh in range(2):
        for z in range(NZ):
            for xl in range(2):
                for y in range(NY):
                    for core in range(2):
                        src = (xh * 4 + z) * 16 + (xl * 4 + y) * 2 + core
                        x2, y2, z2, core2 = move(xh * 2 + xl, y, z, core)
                        x2, y2, z2 = x2 % NX, y2 % NY, z2 % NZ
                        dst = ((x2 // 2) * 4 + z2) * 16 + ((x2 % 2) * 4 + y2) * 2 + core2
                        pairs.append((src, dst))
    return lax.ppermute(a, AXES, pairs)


def send_first(a, d):
    return _send(a, lambda x, y, z, c: (x, y + d, z, c) if c == 0 else (x + d, y, z, c))


def send_second(a, d):
    return _send(a, lambda x, y, z, c: (x + d, y, z, c) if c == 0 else (x, y + d, z, c))


def send_core(a):
    return _send(a, lambda x, y, z, c: (x, y, z, 1 - c))


def send_z(a, d):
    return _send(a, lambda x, y, z, c: (x, y, z + d, c))


def send_far(a):
    return _send(a, lambda x, y, z, c: (x + 2, y, z, c))


def _params(mib):
    return pltpu.CompilerParams(vmem_limit_bytes=mib << 20)


def _load_kernel(dp_ref, c_ref, half_ref, o_ref, sems):
    k = half_ref.shape[0]
    n = sems.shape[0]
    step = k // n
    base = (dp_ref[0] // NZ) * k
    copies = []
    for j in range(n):
        src = c_ref.at[pl.ds(pl.multiple_of(base + j * step, step), step), :]
        dst = half_ref.at[pl.ds(j * step, step), :]
        copies.append(pltpu.make_async_copy(src, dst, sems.at[j]))
        copies[-1].start()
    for j in range(n):
        copies[j].wait()
        rows = slice(j * step, (j + 1) * step)
        v = half_ref[rows, :].astype(F32)
        s = 0.5 * jnp.sum(v * v, axis=1, keepdims=True)
        o_ref[rows, :] = jnp.broadcast_to(s, (step, 128))


def load_half(dp, cents):
    k, d = cents.shape[0] // 2, cents.shape[1]
    return pl.pallas_call(
        _load_kernel,
        out_shape=(
            jax.ShapeDtypeStruct((k, d), BF16),
            jax.ShapeDtypeStruct((k, 128), F32),
        ),
        in_specs=[SMEM, pl.BlockSpec(memory_space=pltpu.HBM)],
        out_specs=(VMEM, VMEM),
        scratch_shapes=[pltpu.SemaphoreType.DMA((8,))],
        compiler_params=_params(4),
        cost_estimate=pl.CostEstimate(
            flops=2 * k * d, bytes_accessed=k * d * 2, transcendentals=0
        ),
        name="load_half",
    )(dp, cents)


def _join_kernel(*refs):
    pos = 0
    for r in refs[:2]:
        n = r.shape[0]
        refs[-1][pos : pos + n, :] = r[...]
        pos += n


def join(a, b, *after):
    parts = (a, b, *after)
    rows, d = a.shape[0] + b.shape[0], a.shape[1]
    return pl.pallas_call(
        _join_kernel,
        out_shape=jax.ShapeDtypeStruct((rows, d), parts[0].dtype),
        in_specs=[VMEM] * len(parts),
        out_specs=VMEM,
        compiler_params=_params(2),
        name="join",
    )(*parts)


def _block(dp, n):
    xh = (dp // NZ + 1 - n // NZ) % 2
    return xh * NZ + (dp + SHIFTS[n % NZ]) % NZ


def _score_kernel(gain, n_x, dp_ref, *refs):
    x_refs = refs[:n_x]
    c_refs, h_refs = refs[n_x : n_x + 2], refs[n_x + 2 : n_x + 4]
    w_ref, st_ref, xp_ref, u_ref, xt_ref = refs[-5:]
    k = h_refs[0].shape[0]
    r = w_ref.shape[2]
    kb = 256
    pos = 0
    for x_ref in x_refs:
        n = x_ref.shape[0]
        xt_ref[:, pos : pos + n] = x_ref[...].T
        pos += n

    def dots(b, j):
        rows = slice(j * kb, (j + 1) * kb)
        u = jnp.dot(c_refs[b][rows, :], xt_ref[...], preferred_element_type=F32)
        u = u - jnp.tile(h_refs[b][rows, :], (1, r // 128))
        u_ref[b, rows, :] = u
        return jnp.max(u, axis=0, keepdims=True)

    def weights(b, j, m):
        rows = slice(j * kb, (j + 1) * kb)
        w = jnp.exp2((u_ref[b, rows, :] - m) * gain)
        w_ref[b, rows, :] = w.astype(BF16)
        return jnp.sum(w, axis=0, keepdims=True)

    def largest(ms):
        return functools.reduce(jnp.maximum, ms)

    nj = k // kb
    m0 = largest([dots(0, j) for j in range(nj)])
    ms, ss = [], []
    for j in range(nj):
        ms.append(dots(1, j))
        ss.append(weights(0, j, m0))
    m1 = largest(ms)
    st_ref[0:1, :] = m0
    st_ref[1:2, :] = sum(ss)
    for f in range(2 * NZ):
        off = pl.multiple_of(_block(dp_ref[0], f) * 128, 128)
        pos = 0
        for x_ref in x_refs:
            n = x_ref.shape[0]
            xp_ref[pos : pos + n, f * 128 : (f + 1) * 128] = x_ref[:, pl.ds(off, 128)]
            pos += n
    st_ref[2:3, :] = m1
    st_ref[3:4, :] = sum([weights(1, j, m1) for j in range(nj)])
    st_ref[4:8, :] = jnp.zeros((4, r), F32)


def score(dp, xs, cents, norms, gain, after):
    r, d = sum(x.shape[0] for x in xs), xs[0].shape[1]
    k = norms[0].shape[0]
    return pl.pallas_call(
        functools.partial(_score_kernel, gain, len(xs)),
        out_shape=(
            jax.ShapeDtypeStruct((2, k, r), BF16),
            jax.ShapeDtypeStruct((8, r), F32),
            jax.ShapeDtypeStruct((r, d), BF16),
        ),
        in_specs=[SMEM] + [VMEM] * (len(xs) + 4 + len(after)),
        out_specs=(VMEM, VMEM, VMEM),
        scratch_shapes=[pltpu.VMEM((2, k, r), F32), pltpu.VMEM((d, r), BF16)],
        compiler_params=_params(14),
        cost_estimate=pl.CostEstimate(
            flops=8 * r * k * d, bytes_accessed=2 * r * d, transcendentals=2 * r * k
        ),
        name="score",
    )(dp, *xs, *cents, *norms, *after)


def _sum_kernel(half, group, n_arr, has_add, *refs):
    w_refs, x_refs, sc_refs = refs[:n_arr], refs[n_arr : 2 * n_arr], refs[2 * n_arr]
    pos = 2 * n_arr + 1
    add_ref = refs[pos] if has_add else None
    outs = refs[pos + 1 if has_add else pos : -1]
    cnt_ref = refs[-1]
    k, r = w_refs[0].shape[1:]
    kb = 256
    per = kb // 128
    n_blk = NZ
    cols = slice(group * n_blk * 128, (group + 1) * n_blk * 128)

    def put(f, rows, v):
        if has_add:
            outs[f][rows, :] = v
        else:
            outs[0][f, rows, :] = v

    for j in range(k // kb):
        rows = slice(j * kb, (j + 1) * kb)
        acc, lanes = None, None
        for a in range(n_arr):
            sc = sc_refs[half : half + 1, a * r : (a + 1) * r]
            w = (w_refs[a][half, rows, :].astype(F32) * sc).astype(BF16)
            wf = w.astype(F32)
            for t in range(r // 128):
                part = wf[:, t * 128 : (t + 1) * 128]
                lanes = part if lanes is None else lanes + part
            d = jnp.dot(w, x_refs[a][:, cols], preferred_element_type=F32)
            acc = d if acc is None else acc + d
        col = jnp.sum(lanes.T, axis=0, keepdims=True)
        for t in range(per):
            cnt_ref[j * per + t : j * per + t + 1, :] = col[:, t * 128 : (t + 1) * 128]
        for f in range(n_blk):
            v = acc[:, f * 128 : (f + 1) * 128]
            if has_add:
                v = v + add_ref[f, rows, :].astype(F32)
            put(f, rows, v.astype(BF16))
    c = cnt_ref[...]
    if has_add:
        c = c + _unpack_counts(add_ref[0, k : k + COUNT_ROWS, :])
    packed = _pack_counts(c)
    for f in range(n_blk):
        put(f, slice(k, k + COUNT_ROWS), packed)


def _pack_counts(c):
    hi = c.astype(BF16).astype(F32)
    mid = (c - hi).astype(BF16).astype(F32)
    lo = (c - hi) - mid
    return jnp.concatenate([hi, mid, lo, jnp.zeros_like(lo)], axis=0).astype(BF16)


def _unpack_counts(rows):
    t = rows.astype(F32)
    return (t[0:8] + t[8:16]) + t[16:24]


def weighted_sums(half, group, ws, xs, scales, add=None):
    n_arr = len(ws)
    k, r = ws[0].shape[1:]
    rows = k + COUNT_ROWS
    operands = [*ws, *xs, scales]
    if add is None:
        out_shape = [jax.ShapeDtypeStruct((NZ, rows, 128), BF16)]
    else:
        operands.append(add)
        out_shape = [jax.ShapeDtypeStruct((rows, 128), BF16)] * NZ
    return pl.pallas_call(
        functools.partial(_sum_kernel, half, group, n_arr, add is not None),
        out_shape=out_shape,
        in_specs=[VMEM] * len(operands),
        out_specs=[VMEM] * len(out_shape),
        scratch_shapes=[pltpu.VMEM((8, 128), F32)],
        compiler_params=_params(14),
        cost_estimate=pl.CostEstimate(
            flops=4 * k * n_arr * r * NZ * 128, bytes_accessed=2 * rows * NZ * 128,
            transcendentals=0,
        ),
        name="sums_sib" if add is None else "sums_own",
    )(*operands)


def _total(parts):
    total = None
    for p in parts:
        v = p[...].astype(F32)
        total = v if total is None else total + v
    return total


def _add_kernel(*refs):
    o_ref = refs[-1]
    k = o_ref.shape[0] - COUNT_ROWS
    total = _total(refs[:-1])
    o_ref[:k, :] = total[:k].astype(BF16)
    o_ref[k:, :] = _pack_counts(_unpack_counts(total[k:]))


def add_blocks(parts):
    return pl.pallas_call(
        _add_kernel,
        out_shape=jax.ShapeDtypeStruct(parts[0].shape, BF16),
        in_specs=[VMEM] * len(parts),
        out_specs=VMEM,
        compiler_params=_params(8),
        cost_estimate=pl.CostEstimate(
            flops=0, bytes_accessed=10 * parts[0].size, transcendentals=0
        ),
        name="add_blocks",
    )(*parts)


def _final_kernel(n, dp_ref, *refs):
    parts = (refs[:n], refs[n : n + 1])
    c_ref, o_ref = refs[n + 1 :]
    k = c_ref.shape[0] // 2
    for j in range(2):
        side = dp_ref[0] // NZ if j == 0 else 1 - dp_ref[0] // NZ
        off = pl.multiple_of(side * k, k)
        total = _total(parts[j])
        c = _unpack_counts(total[k:])
        cnt = jnp.concatenate([c[q : q + 1, :] for q in range(k // 128)], axis=1)
        cols = pl.ds(pl.multiple_of(dp_ref[0] * 128, 128), 128)
        top = total[:k] + PRIOR * c_ref[pl.ds(off, k), cols].astype(F32)
        o_ref[:, pl.ds(off, k)] = top.T / (cnt + PRIOR)


def finish(dp, mine, other, centroids):
    return pl.pallas_call(
        functools.partial(_final_kernel, len(mine)),
        out_shape=jax.ShapeDtypeStruct((128, centroids.shape[0]), F32),
        in_specs=[SMEM] + [VMEM] * (len(mine) + 2),
        out_specs=VMEM,
        compiler_params=_params(12),
        name="finish",
    )(dp, *mine, other, centroids)


def _slots():
    place = {}
    for a in range(4):
        place[0, a] = (0, a * 128)
        place[2, a] = (3, a * 128)
        place[1, a] = (1 if a < 2 else 2, (a % 2) * 128)
        place[3, a] = (1 if a >= 2 else 2, 256 + (a % 2) * 128)
    return [place[b, a] for b in range(4) for a in range(4)]


def _gather_slots(refs, row):
    return jnp.concatenate(
        [refs[n][row : row + 1, off : off + 128] for n, off in _slots()], axis=0
    )


def _merge(pairs, gain):
    m = functools.reduce(jnp.maximum, [p[0] for p in pairs])
    s = sum(p[1] * jnp.exp2((p[0] - m) * gain) for p in pairs)
    return m, s


def _shifted(v, d, axis):
    if d == 0:
        return v
    if axis == 1:
        return jnp.concatenate([v[16 - 4 * d :], v[: 16 - 4 * d]], axis=0)
    parts = []
    for b in range(0, 16, 4):
        parts += [v[b + 4 - d : b + 4], v[b : b + 4 - d]]
    return jnp.concatenate(parts, axis=0)


def _pack_kernel(gain, *refs):
    o_ref = refs[-1]
    pairs = [(_gather_slots(refs, 2 * b), _gather_slots(refs, 2 * b + 1)) for b in range(2)]
    o_ref[0], o_ref[1] = _merge(pairs, gain)


def _merge_kernel(gain, axis, *refs):
    o_ref = refs[-1]
    pairs = [
        (_shifted(refs[d][0], d, axis), _shifted(refs[d][1], d, axis)) for d in range(4)
    ]
    o_ref[0], o_ref[1] = _merge(pairs, gain)


def _scale_kernel(gain, axis, *refs):
    stats, o_ref = refs[4:8], refs[-1]
    pairs = [
        (_shifted(refs[d][0], d, axis), _shifted(refs[d][1], d, axis)) for d in range(4)
    ]
    top, total = _merge(pairs, gain)
    r = stats[0].shape[1]
    for b in range(2):
        q = jnp.exp2((_gather_slots(stats, 2 * b) - top) * gain) / total
        for i, (n, off) in enumerate(_slots()):
            o_ref[b : b + 1, n * r + off : n * r + off + 128] = q[i : i + 1, :]


def _small(kernel, shape, args, name):
    return pl.pallas_call(
        kernel,
        out_shape=jax.ShapeDtypeStruct(shape, F32),
        in_specs=[VMEM] * len(args),
        out_specs=VMEM,
        compiler_params=_params(2),
        name=name,
    )(*args)


def local(points, centroids):
    features = points.shape[1]
    gain = BETA_GAIN * features ** (-0.5) * math.log2(math.e)
    dp = lax.axis_index("dp").astype(jnp.int32).reshape(1)

    shards = [points] + [send_first(points, d) for d in (1, 2, 3)]
    whole = (centroids, send_core(centroids))
    own, own_norm = load_half(dp, whole[0])
    line_a, line_b = join(shards[0], shards[1], own_norm), join(shards[2], shards[3], own_norm)
    half = line_a.shape[0]
    up_a, down_b = send_second(line_a, 1), send_second(line_b, 3)
    sib, sib_norm = load_half(dp, whole[1])
    cents = (own, sib)
    late_a, late_b, sib_norm = lax.optimization_barrier((line_a, line_b, sib_norm))
    norms = (own_norm, sib_norm)
    up_b, down_a = send_second(late_b, 1), send_second(late_a, 3)

    ws, stats, xs = [], [], []

    def run(*xin):
        w, st, xp = score(dp, xin, cents, norms, gain, stats[-1:])
        ws.append(w)
        stats.append(st)
        xs.append(xp)

    run(line_a, line_b)
    up_a, down_b, stats[0] = lax.optimization_barrier((up_a, down_b, stats[0]))
    far_a, far_b = send_second(up_a, 1), send_second(down_b, 3)
    run(up_a, down_b)
    run(up_b, down_a)
    run(far_a, far_b)

    shape = (2, 16, 128)
    pack = _small(functools.partial(_pack_kernel, gain), shape, stats, "stats_pack")
    every = [pack] + [send_first(pack, d) for d in (1, 2, 3)]
    pack = _small(functools.partial(_merge_kernel, gain, 0), shape, every, "stats_merge")
    every = [pack] + [send_second(pack, d) for d in (1, 2, 3)]
    scales = _small(
        functools.partial(_scale_kernel, gain, 1),
        (8, sum(st.shape[1] for st in stats)),
        every + stats,
        "stats_scale",
    )

    swapped = [send_core(weighted_sums(1, g, ws, xs, scales)[0]) for g in range(2)]
    got = []
    for g in range(2):
        sums = weighted_sums(0, g, ws, xs, scales, add=swapped[g])
        got.append([sums[3]] + [send_z(sums[n], d) for n, d in enumerate(SHIFTS[:3])])
    other = send_far(add_blocks(got[0]))
    return finish(dp, got[1], other, centroids)


def solution(mesh):
    return jax.shard_map(
        local,
        mesh=mesh,
        in_specs=(P(("dp", "cent"), None), P("cent", None)),
        out_specs=P("dp", "cent"),
        check_vma=False,
    )
```

```python
import functools
import math

import jax
import jax.numpy as jnp
from jax import lax
from jax.experimental import pallas as pl
from jax.experimental.pallas import tpu as pltpu
from jax.sharding import PartitionSpec as P

BETA_GAIN = 4.0
PRIOR = 0.5
F32 = jnp.float32
BF16 = jnp.bfloat16

NX, NY, NZ = 4, 4, 4
AXES = ("dp", "cent")
COUNT_ROWS = 32
LIGHT = pl.CostEstimate(flops=1024, bytes_accessed=1024, transcendentals=0)
COSTS = (pl.CostEstimate(flops=40 << 30, bytes_accessed=1024, transcendentals=0), LIGHT)
SHIFTS = (2, 1, 3, 0)
VMEM = pl.BlockSpec(memory_space=pltpu.VMEM)
SMEM = pl.BlockSpec(memory_space=pltpu.SMEM)


def _send(a, move):
    pairs = []
    for xh in range(2):
        for z in range(NZ):
            for xl in range(2):
                for y in range(NY):
                    for core in range(2):
                        src = (xh * 4 + z) * 16 + (xl * 4 + y) * 2 + core
                        x2, y2, z2, core2 = move(xh * 2 + xl, y, z, core)
                        x2, y2, z2 = x2 % NX, y2 % NY, z2 % NZ
                        dst = ((x2 // 2) * 4 + z2) * 16 + ((x2 % 2) * 4 + y2) * 2 + core2
                        pairs.append((src, dst))
    return lax.ppermute(a, AXES, pairs)


def send_first(a, d):
    return _send(a, lambda x, y, z, c: (x, y + d, z, c) if c == 0 else (x + d, y, z, c))


def send_second(a, d):
    return _send(a, lambda x, y, z, c: (x + d, y, z, c) if c == 0 else (x, y + d, z, c))


def send_core(a):
    return _send(a, lambda x, y, z, c: (x, y, z, 1 - c))


def send_z(a, d):
    return _send(a, lambda x, y, z, c: (x, y, z + d, c))


def send_far(a):
    return _send(a, lambda x, y, z, c: (x + 2, y, z, c))


def _params(mib):
    return pltpu.CompilerParams(vmem_limit_bytes=mib << 20)


def _load_kernel(dp_ref, c_ref, half_ref, o_ref, sems):
    k = half_ref.shape[0]
    n = sems.shape[0]
    step = k // n
    base = (dp_ref[0] // NZ) * k
    copies = []
    for j in range(n):
        src = c_ref.at[pl.ds(pl.multiple_of(base + j * step, step), step), :]
        dst = half_ref.at[pl.ds(j * step, step), :]
        copies.append(pltpu.make_async_copy(src, dst, sems.at[j]))
        copies[-1].start()
    for j in range(n):
        copies[j].wait()
        rows = slice(j * step, (j + 1) * step)
        v = half_ref[rows, :].astype(F32)
        s = 0.5 * jnp.sum(v * v, axis=1, keepdims=True)
        o_ref[rows, :] = jnp.broadcast_to(s, (step, 128))


def load_half(dp, cents, mib):
    k, d = cents.shape[0] // 2, cents.shape[1]
    return pl.pallas_call(
        _load_kernel,
        out_shape=(
            jax.ShapeDtypeStruct((k, d), BF16),
            jax.ShapeDtypeStruct((k, 128), F32),
        ),
        in_specs=[SMEM, pl.BlockSpec(memory_space=pltpu.HBM)],
        out_specs=(VMEM, VMEM),
        scratch_shapes=[pltpu.SemaphoreType.DMA((8,))],
        compiler_params=_params(mib),
        cost_estimate=LIGHT,
        name="load_half",
    )(dp, cents)


def _join_kernel(*refs):
    pos = 0
    for r in refs[:2]:
        n = r.shape[0]
        refs[-1][pos : pos + n, :] = r[...]
        pos += n


def join(a, b, *after):
    parts = (a, b, *after)
    rows, d = a.shape[0] + b.shape[0], a.shape[1]
    return pl.pallas_call(
        _join_kernel,
        out_shape=jax.ShapeDtypeStruct((rows, d), parts[0].dtype),
        in_specs=[VMEM] * len(parts),
        out_specs=VMEM,
        compiler_params=_params(2),
        name="join",
    )(*parts)


def _block(dp, n):
    xh = (dp // NZ + 1 - n // NZ) % 2
    return xh * NZ + (dp + SHIFTS[n % NZ]) % NZ


def _score_kernel(gain, n_x, dp_ref, *refs):
    x_refs = refs[:n_x]
    c_refs, h_refs = refs[n_x : n_x + 2], refs[n_x + 2 : n_x + 4]
    w_ref, st_ref, xp_ref, u_ref, xt_ref = refs[-5:]
    k = h_refs[0].shape[0]
    r = w_ref.shape[2]
    kb = 256
    pos = 0
    for x_ref in x_refs:
        n = x_ref.shape[0]
        xt_ref[:, pos : pos + n] = x_ref[...].T
        pos += n

    def dots(b, j):
        rows = slice(j * kb, (j + 1) * kb)
        u = jnp.dot(c_refs[b][rows, :], xt_ref[...], preferred_element_type=F32)
        u = u - jnp.tile(h_refs[b][rows, :], (1, r // 128))
        u_ref[b, rows, :] = u
        return jnp.max(u, axis=0, keepdims=True)

    def weights(b, j, m):
        rows = slice(j * kb, (j + 1) * kb)
        w = jnp.exp2((u_ref[b, rows, :] - m) * gain)
        w_ref[b, rows, :] = w.astype(BF16)
        return jnp.sum(w, axis=0, keepdims=True)

    def largest(ms):
        return functools.reduce(jnp.maximum, ms)

    nj = k // kb
    m0 = largest([dots(0, j) for j in range(nj)])
    ms, ss = [], []
    for j in range(nj):
        ms.append(dots(1, j))
        ss.append(weights(0, j, m0))
    m1 = largest(ms)
    st_ref[0:1, :] = m0
    st_ref[1:2, :] = sum(ss)
    for f in range(2 * NZ):
        off = pl.multiple_of(_block(dp_ref[0], f) * 128, 128)
        pos = 0
        for x_ref in x_refs:
            n = x_ref.shape[0]
            xp_ref[pos : pos + n, f * 128 : (f + 1) * 128] = x_ref[:, pl.ds(off, 128)]
            pos += n
    st_ref[2:3, :] = m1
    st_ref[3:4, :] = sum([weights(1, j, m1) for j in range(nj)])
    st_ref[4:8, :] = jnp.zeros((4, r), F32)


def score(dp, xs, cents, norms, gain, after):
    r, d = sum(x.shape[0] for x in xs), xs[0].shape[1]
    k = norms[0].shape[0]
    return pl.pallas_call(
        functools.partial(_score_kernel, gain, len(xs)),
        out_shape=(
            jax.ShapeDtypeStruct((2, k, r), BF16),
            jax.ShapeDtypeStruct((8, r), F32),
            jax.ShapeDtypeStruct((r, d), BF16),
        ),
        in_specs=[SMEM] + [VMEM] * (len(xs) + 4 + len(after)),
        out_specs=(VMEM, VMEM, VMEM),
        scratch_shapes=[pltpu.VMEM((2, k, r), F32), pltpu.VMEM((d, r), BF16)],
        compiler_params=_params(14),
        cost_estimate=LIGHT,
        name="score",
    )(dp, *xs, *cents, *norms, *after)


def _sum_kernel(half, group, n_arr, *refs):
    w_refs, x_refs, sc_ref = refs[:n_arr], refs[n_arr : 2 * n_arr], refs[2 * n_arr]
    packed = half == 1
    out_ref, cnt_ref = refs[-2:]
    k, r = w_refs[0].shape[1:]
    kb = 256
    per = kb // 128
    cols = slice(group * NZ * 128, (group + 1) * NZ * 128)
    for j in range(k // kb):
        rows = slice(j * kb, (j + 1) * kb)
        acc, lanes = None, None
        for a in range(n_arr):
            sc = sc_ref[half : half + 1, a * r : (a + 1) * r]
            w = (w_refs[a][half, rows, :].astype(F32) * sc).astype(BF16)
            wf = w.astype(F32)
            for t in range(r // 128):
                part = wf[:, t * 128 : (t + 1) * 128]
                lanes = part if lanes is None else lanes + part
            d = jnp.dot(w, x_refs[a][:, cols], preferred_element_type=F32)
            acc = d if acc is None else acc + d
        col = jnp.sum(lanes.T, axis=0, keepdims=True)
        for t in range(per):
            cnt_ref[j * per + t : j * per + t + 1, :] = col[:, t * 128 : (t + 1) * 128]
        for f in range(NZ):
            out_ref[f, rows, :] = acc[:, f * 128 : (f + 1) * 128].astype(out_ref.dtype)
    if packed:
        for f in range(NZ):
            out_ref[f, k:, :] = _pack_counts(cnt_ref[...])


def _pack_counts(c):
    hi = c.astype(BF16).astype(F32)
    mid = (c - hi).astype(BF16).astype(F32)
    lo = (c - hi) - mid
    return jnp.concatenate([hi, mid, lo, jnp.zeros_like(lo)], axis=0).astype(BF16)


def _unpack_counts(rows):
    t = rows.astype(F32)
    return (t[0:8] + t[8:16]) + t[16:24]


COUNTS = jax.ShapeDtypeStruct((8, 128), F32)


def weighted_sums(half, group, ws, xs, scales, after=()):
    n_arr = len(ws)
    k, r = ws[0].shape[1:]
    operands = [*ws, *xs, scales, *after]
    if half == 1:
        out_shape = jax.ShapeDtypeStruct((NZ, k + COUNT_ROWS, 128), BF16)
        out_specs, scratch = VMEM, [pltpu.VMEM((8, 128), F32)]
    else:
        out_shape = (jax.ShapeDtypeStruct((NZ, k, 128), F32), COUNTS)
        out_specs, scratch = (VMEM, VMEM), []
    return pl.pallas_call(
        functools.partial(_sum_kernel, half, group, n_arr),
        out_shape=out_shape,
        in_specs=[VMEM] * len(operands),
        out_specs=out_specs,
        scratch_shapes=scratch,
        compiler_params=_params(14),
        cost_estimate=COSTS[half],
        name="sums_sib" if half else "sums_own",
    )(*operands)


def _call(kernel, out_shape, args, name, mib=8):
    many = isinstance(out_shape, tuple)
    return pl.pallas_call(
        kernel,
        out_shape=out_shape,
        in_specs=[VMEM] * len(args),
        out_specs=(VMEM,) * len(out_shape) if many else VMEM,
        compiler_params=_params(mib),
        cost_estimate=LIGHT,
        name=name,
    )(*args)


def _mix_kernel(acc_ref, cnt_ref, add_ref, *refs):
    keep_ref, sum_ref = refs[-2:]
    outs = refs[-2 - (NZ - 1) : -2]
    k = acc_ref.shape[1]
    c = cnt_ref[...] + _unpack_counts(add_ref[0, k:, :])
    sum_ref[...] = c
    packed = _pack_counts(c)
    for f in range(NZ - 1):
        outs[f][:k, :] = (acc_ref[f] + add_ref[f, :k, :].astype(F32)).astype(BF16)
        outs[f][k:, :] = packed
    keep_ref[...] = acc_ref[NZ - 1] + add_ref[NZ - 1, :k, :].astype(F32)


def mix(acc, cnt, add):
    k = acc.shape[1]
    out = (jax.ShapeDtypeStruct((k + COUNT_ROWS, 128), BF16),) * (NZ - 1)
    out += (jax.ShapeDtypeStruct((k, 128), F32), COUNTS)
    return _call(_mix_kernel, out, [acc, cnt, add], "mix")


def _totals(keep_ref, cnt_ref, refs):
    k = keep_ref.shape[0]
    total, c = keep_ref[...], cnt_ref[...]
    for r in refs:
        total = total + r[:k, :].astype(F32)
        c = c + _unpack_counts(r[k:, :])
    return total, c


def _far_kernel(keep_ref, cnt_ref, *refs):
    o_ref = refs[-1]
    k = keep_ref.shape[0]
    total, c = _totals(keep_ref, cnt_ref, refs[: NZ - 1])
    o_ref[:k, :] = total.astype(BF16)
    o_ref[k:, :] = _pack_counts(c)


def _final_kernel(dp_ref, keep_ref, cnt_ref, *refs):
    other_ref, c_ref, o_ref = refs[-3:]
    k = c_ref.shape[0] // 2
    xh = dp_ref[0] // NZ
    cols = pl.ds(pl.multiple_of(dp_ref[0] * 128, 128), 128)
    mine = _totals(keep_ref, cnt_ref, refs[:-3])
    other = other_ref[:k, :].astype(F32), _unpack_counts(other_ref[k:, :])
    for side, (total, c) in ((xh, mine), (1 - xh, other)):
        off = pl.multiple_of(side * k, k)
        cnt = jnp.concatenate([c[q : q + 1, :] for q in range(k // 128)], axis=1)
        top = total + PRIOR * c_ref[pl.ds(off, k), cols].astype(F32)
        o_ref[:, pl.ds(off, k)] = top.T / (cnt + PRIOR)


def finish(dp, parts, other, centroids):
    return pl.pallas_call(
        _final_kernel,
        out_shape=jax.ShapeDtypeStruct((128, centroids.shape[0]), F32),
        in_specs=[SMEM] + [VMEM] * (len(parts) + 2),
        out_specs=VMEM,
        compiler_params=_params(12),
        name="finish",
    )(dp, *parts, other, centroids)


def _slots():
    place = {}
    for a in range(4):
        place[0, a] = (0, a * 128)
        place[2, a] = (3, a * 128)
        place[1, a] = (1 if a < 2 else 2, (a % 2) * 128)
        place[3, a] = (1 if a >= 2 else 2, 256 + (a % 2) * 128)
    return [place[b, a] for b in range(4) for a in range(4)]


def _gather_slots(refs, row):
    return jnp.concatenate(
        [refs[n][row : row + 1, off : off + 128] for n, off in _slots()], axis=0
    )


def _merge(pairs, gain):
    m = functools.reduce(jnp.maximum, [p[0] for p in pairs])
    s = sum(p[1] * jnp.exp2((p[0] - m) * gain) for p in pairs)
    return m, s


def _shifted(v, d, axis):
    if d == 0:
        return v
    if axis == 1:
        return jnp.concatenate([v[16 - 4 * d :], v[: 16 - 4 * d]], axis=0)
    parts = []
    for b in range(0, 16, 4):
        parts += [v[b + 4 - d : b + 4], v[b : b + 4 - d]]
    return jnp.concatenate(parts, axis=0)


def _pack_kernel(gain, *refs):
    o_ref = refs[-1]
    pairs = [(_gather_slots(refs, 2 * b), _gather_slots(refs, 2 * b + 1)) for b in range(2)]
    o_ref[0], o_ref[1] = _merge(pairs, gain)


def _merge_kernel(gain, axis, *refs):
    o_ref = refs[-1]
    pairs = [
        (_shifted(refs[d][0], d, axis), _shifted(refs[d][1], d, axis)) for d in range(4)
    ]
    o_ref[0], o_ref[1] = _merge(pairs, gain)


def _scale_kernel(gain, axis, *refs):
    stats, o_ref = refs[4:8], refs[-1]
    pairs = [
        (_shifted(refs[d][0], d, axis), _shifted(refs[d][1], d, axis)) for d in range(4)
    ]
    top, total = _merge(pairs, gain)
    r = stats[0].shape[1]
    for b in range(2):
        q = jnp.exp2((_gather_slots(stats, 2 * b) - top) * gain) / total
        for i, (n, off) in enumerate(_slots()):
            o_ref[b : b + 1, n * r + off : n * r + off + 128] = q[i : i + 1, :]


def local(points, centroids):
    features = points.shape[1]
    gain = BETA_GAIN * features ** (-0.5) * math.log2(math.e)
    dp = lax.axis_index("dp").astype(jnp.int32).reshape(1)

    shards = [points] + [send_first(points, d) for d in (1, 2, 3)]
    whole = (centroids, send_core(centroids))
    own, own_norm = load_half(dp, whole[0], 4)
    line_a, line_b = join(shards[0], shards[1], own_norm), join(shards[2], shards[3], own_norm)
    half = line_a.shape[0]
    up_a, down_b = send_second(line_a, 1), send_second(line_b, 3)
    sib, sib_norm = load_half(dp, whole[1], 4)
    cents = (own, sib)
    late_a, late_b, sib_norm = lax.optimization_barrier((line_a, line_b, sib_norm))
    norms = (own_norm, sib_norm)
    up_b, down_a = send_second(late_b, 1), send_second(late_a, 3)

    ws, stats, xs = [], [], []

    def run(*xin):
        w, st, xp = score(dp, xin, cents, norms, gain, stats[-1:])
        ws.append(w)
        stats.append(st)
        xs.append(xp)

    run(line_a, line_b)
    up_a, down_b, stats[0] = lax.optimization_barrier((up_a, down_b, stats[0]))
    far_a, far_b = send_second(up_a, 1), send_second(down_b, 3)
    run(up_a, down_b)
    run(up_b, down_a)
    run(far_a, far_b)

    shape = jax.ShapeDtypeStruct((2, 16, 128), F32)
    pack = _call(functools.partial(_pack_kernel, gain), shape, stats, "stats_pack", 2)
    every = [pack] + [send_first(pack, d) for d in (1, 2, 3)]
    pack = _call(functools.partial(_merge_kernel, gain, 0), shape, every, "stats_merge", 2)
    every = [pack] + [send_second(pack, d) for d in (1, 2, 3)]
    scales = _call(
        functools.partial(_scale_kernel, gain, 1),
        jax.ShapeDtypeStruct((8, sum(st.shape[1] for st in stats)), F32),
        every + stats,
        "stats_scale",
        2,
    )

    got, order = [], []
    for g in range(2):
        part = send_core(weighted_sums(1, g, ws, xs, scales, order))
        acc, cnt = weighted_sums(0, g, ws, xs, scales, order)
        *blocks, keep, cnt = mix(acc, cnt, part)
        order = [cnt]
        got.append([keep, cnt] + [send_z(v, d) for v, d in zip(blocks, SHIFTS)])
    rows = jax.ShapeDtypeStruct(blocks[0].shape, BF16)
    other = send_far(_call(_far_kernel, rows, got[0] + order, "far_sum"))
    return finish(dp, got[1], other, centroids)


def solution(mesh):
    return jax.shard_map(
        local,
        mesh=mesh,
        in_specs=(P(("dp", "cent"), None), P("cent", None)),
        out_specs=P("dp", "cent"),
        check_vma=False,
    )
```

```python
import functools
import math

import jax
import jax.numpy as jnp
from jax import lax
from jax.experimental import pallas as pl
from jax.experimental.pallas import tpu as pltpu
from jax.sharding import PartitionSpec as P

BETA_GAIN = 4.0
PRIOR = 0.5
F32 = jnp.float32
BF16 = jnp.bfloat16

NX, NY, NZ = 4, 4, 4
AXES = ("dp", "cent")
COUNT_ROWS = 32
LIGHT = pl.CostEstimate(flops=1024, bytes_accessed=1024, transcendentals=0)
COSTS = (pl.CostEstimate(flops=40 << 30, bytes_accessed=1024, transcendentals=0), LIGHT)
SHIFTS = (2, 1, 3, 0)
VMEM = pl.BlockSpec(memory_space=pltpu.VMEM)
SMEM = pl.BlockSpec(memory_space=pltpu.SMEM)


def _send(a, move):
    pairs = []
    for xh in range(2):
        for z in range(NZ):
            for xl in range(2):
                for y in range(NY):
                    for core in range(2):
                        src = (xh * 4 + z) * 16 + (xl * 4 + y) * 2 + core
                        x2, y2, z2, core2 = move(xh * 2 + xl, y, z, core)
                        x2, y2, z2 = x2 % NX, y2 % NY, z2 % NZ
                        dst = ((x2 // 2) * 4 + z2) * 16 + ((x2 % 2) * 4 + y2) * 2 + core2
                        pairs.append((src, dst))
    return lax.ppermute(a, AXES, pairs)


def send_first(a, d):
    return _send(a, lambda x, y, z, c: (x, y + d, z, c) if c == 0 else (x + d, y, z, c))


def send_second(a, d):
    return _send(a, lambda x, y, z, c: (x + d, y, z, c) if c == 0 else (x, y + d, z, c))


def send_core(a):
    return _send(a, lambda x, y, z, c: (x, y, z, 1 - c))


def send_z(a, d):
    return _send(a, lambda x, y, z, c: (x, y, z + d, c))


def send_far(a):
    return _send(a, lambda x, y, z, c: (x + 2, y, z, c))


def _params(mib):
    return pltpu.CompilerParams(vmem_limit_bytes=mib << 20)


def _load_kernel(id_ref, c_ref, half_ref, o_ref, sems):
    k = half_ref.shape[0]
    n = sems.shape[0]
    step = k // n
    base = (_dp(id_ref) // NZ) * k
    copies = []
    for j in range(n):
        src = c_ref.at[pl.ds(pl.multiple_of(base + j * step, step), step), :]
        dst = half_ref.at[pl.ds(j * step, step), :]
        copies.append(pltpu.make_async_copy(src, dst, sems.at[j]))
        copies[-1].start()
    for j in range(n):
        copies[j].wait()
        rows = slice(j * step, (j + 1) * step)
        v = half_ref[rows, :].astype(F32)
        s = 0.5 * jnp.sum(v * v, axis=1, keepdims=True)
        o_ref[rows, :] = jnp.broadcast_to(s, (step, 128))


def load_half(ident, cents, mib):
    k, d = cents.shape[0] // 2, cents.shape[1]
    return pl.pallas_call(
        _load_kernel,
        out_shape=(
            jax.ShapeDtypeStruct((k, d), BF16),
            jax.ShapeDtypeStruct((k, 128), F32),
        ),
        in_specs=[SMEM, pl.BlockSpec(memory_space=pltpu.HBM)],
        out_specs=(VMEM, VMEM),
        scratch_shapes=[pltpu.SemaphoreType.DMA((8,))],
        compiler_params=_params(mib),
        cost_estimate=LIGHT,
        name="load_half",
    )(ident, cents)


def _join_kernel(*refs):
    pos = 0
    for r in refs[:2]:
        n = r.shape[0]
        refs[-1][pos : pos + n, :] = r[...]
        pos += n


def join(a, b, *after):
    parts = (a, b, *after)
    rows, d = a.shape[0] + b.shape[0], a.shape[1]
    return pl.pallas_call(
        _join_kernel,
        out_shape=jax.ShapeDtypeStruct((rows, d), parts[0].dtype),
        in_specs=[VMEM] * len(parts),
        out_specs=VMEM,
        compiler_params=_params(2),
        name="join",
    )(*parts)


def _dp(id_ref):
    return id_ref[0] // 16


def _block(dp, n):
    xh = (dp // NZ + 1 - n // NZ) % 2
    return xh * NZ + (dp + SHIFTS[n % NZ]) % NZ


def _score_kernel(gain, n_x, id_ref, *refs):
    x_refs = refs[:n_x]
    c_refs, h_refs = refs[n_x : n_x + 2], refs[n_x + 2 : n_x + 4]
    w_ref, st_ref, xp_ref, u_ref, x_all_ref = refs[-5:]
    k = h_refs[0].shape[0]
    r = w_ref.shape[2]
    kb = 256
    pos = 0
    for x_ref in x_refs:
        n = x_ref.shape[0]
        x_all_ref[pos : pos + n, :] = x_ref[...]
        pos += n

    def dots(b, j):
        rows = slice(j * kb, (j + 1) * kb)
        u = lax.dot_general(
            c_refs[b][rows, :], x_all_ref[...], (((1,), (1,)), ((), ())), preferred_element_type=F32
        )
        u = u - jnp.tile(h_refs[b][rows, :], (1, r // 128))
        u_ref[b, rows, :] = u
        return jnp.max(u, axis=0, keepdims=True)

    def weights(b, j, m):
        rows = slice(j * kb, (j + 1) * kb)
        w = jnp.exp2((u_ref[b, rows, :] - m) * gain)
        w_ref[b, rows, :] = w.astype(BF16)
        return jnp.sum(w, axis=0, keepdims=True)

    def largest(ms):
        return functools.reduce(jnp.maximum, ms)

    nj = k // kb
    m0 = largest([dots(0, j) for j in range(nj)])
    ms, ss = [], []
    for j in range(nj):
        ms.append(dots(1, j))
        ss.append(weights(0, j, m0))
    m1 = largest(ms)
    st_ref[0:1, :] = m0
    st_ref[1:2, :] = sum(ss)
    for f in range(2 * NZ):
        off = pl.multiple_of(_block(_dp(id_ref), f) * 128, 128)
        pos = 0
        for x_ref in x_refs:
            n = x_ref.shape[0]
            xp_ref[pos : pos + n, f * 128 : (f + 1) * 128] = x_ref[:, pl.ds(off, 128)]
            pos += n
    st_ref[2:3, :] = m1
    st_ref[3:4, :] = sum([weights(1, j, m1) for j in range(nj)])
    st_ref[4:8, :] = jnp.zeros((4, r), F32)


def score(ident, xs, cents, norms, gain, after):
    r, d = sum(x.shape[0] for x in xs), xs[0].shape[1]
    k = norms[0].shape[0]
    return pl.pallas_call(
        functools.partial(_score_kernel, gain, len(xs)),
        out_shape=(
            jax.ShapeDtypeStruct((2, k, r), BF16),
            jax.ShapeDtypeStruct((8, r), F32),
            jax.ShapeDtypeStruct((r, d), BF16),
        ),
        in_specs=[SMEM] + [VMEM] * (len(xs) + 4 + len(after)),
        out_specs=(VMEM, VMEM, VMEM),
        scratch_shapes=[pltpu.VMEM((2, k, r), F32), pltpu.VMEM((r, d), BF16)],
        compiler_params=_params(14),
        cost_estimate=LIGHT,
        name="score",
    )(ident, *xs, *cents, *norms, *after)


def _sum_kernel(half, group, n_arr, *refs):
    w_refs, x_refs, sc_ref = refs[:n_arr], refs[n_arr : 2 * n_arr], refs[2 * n_arr]
    packed = half == 1
    out_ref, cnt_ref = refs[-2:]
    k, r = w_refs[0].shape[1:]
    kb = 256
    per = kb // 128
    cols = slice(group * NZ * 128, (group + 1) * NZ * 128)
    for j in range(k // kb):
        rows = slice(j * kb, (j + 1) * kb)
        acc, lanes = None, None
        for a in range(n_arr):
            sc = sc_ref[half : half + 1, a * r : (a + 1) * r]
            w = (w_refs[a][half, rows, :].astype(F32) * sc).astype(BF16)
            wf = w.astype(F32)
            for t in range(r // 128):
                part = wf[:, t * 128 : (t + 1) * 128]
                lanes = part if lanes is None else lanes + part
            d = jnp.dot(w, x_refs[a][:, cols], preferred_element_type=F32)
            acc = d if acc is None else acc + d
        col = jnp.sum(lanes.T, axis=0, keepdims=True)
        for t in range(per):
            cnt_ref[j * per + t : j * per + t + 1, :] = col[:, t * 128 : (t + 1) * 128]
        for f in range(NZ):
            out_ref[f, rows, :] = acc[:, f * 128 : (f + 1) * 128].astype(out_ref.dtype)
    if packed:
        for f in range(NZ):
            out_ref[f, k:, :] = _pack_counts(cnt_ref[...])


def _pack_counts(c):
    hi = c.astype(BF16).astype(F32)
    mid = (c - hi).astype(BF16).astype(F32)
    lo = (c - hi) - mid
    return jnp.concatenate([hi, mid, lo, jnp.zeros_like(lo)], axis=0).astype(BF16)


def _unpack_counts(rows):
    t = rows.astype(F32)
    return (t[0:8] + t[8:16]) + t[16:24]


COUNTS = jax.ShapeDtypeStruct((8, 128), F32)


def weighted_sums(half, group, ws, xs, scales, after=()):
    n_arr = len(ws)
    k, r = ws[0].shape[1:]
    operands = [*ws, *xs, scales, *after]
    if half == 1:
        out_shape = jax.ShapeDtypeStruct((NZ, k + COUNT_ROWS, 128), BF16)
        out_specs, scratch = VMEM, [pltpu.VMEM((8, 128), F32)]
    else:
        out_shape = (jax.ShapeDtypeStruct((NZ, k, 128), F32), COUNTS)
        out_specs, scratch = (VMEM, VMEM), []
    return pl.pallas_call(
        functools.partial(_sum_kernel, half, group, n_arr),
        out_shape=out_shape,
        in_specs=[VMEM] * len(operands),
        out_specs=out_specs,
        scratch_shapes=scratch,
        compiler_params=_params(14),
        cost_estimate=COSTS[half],
        name="sums_sib" if half else "sums_own",
    )(*operands)


def _call(kernel, out_shape, args, name, mib=8):
    many = isinstance(out_shape, tuple)
    return pl.pallas_call(
        kernel,
        out_shape=out_shape,
        in_specs=[VMEM] * len(args),
        out_specs=(VMEM,) * len(out_shape) if many else VMEM,
        compiler_params=_params(mib),
        cost_estimate=LIGHT,
        name=name,
    )(*args)


def _mix_kernel(acc_ref, cnt_ref, add_ref, *refs):
    keep_ref, sum_ref = refs[-2:]
    outs = refs[-2 - (NZ - 1) : -2]
    k = acc_ref.shape[1]
    c = cnt_ref[...] + _unpack_counts(add_ref[0, k:, :])
    sum_ref[...] = c
    packed = _pack_counts(c)
    for f in range(NZ - 1):
        outs[f][:k, :] = (acc_ref[f] + add_ref[f, :k, :].astype(F32)).astype(BF16)
        outs[f][k:, :] = packed
    keep_ref[...] = acc_ref[NZ - 1] + add_ref[NZ - 1, :k, :].astype(F32)


def mix(acc, cnt, add):
    k = acc.shape[1]
    out = (jax.ShapeDtypeStruct((k + COUNT_ROWS, 128), BF16),) * (NZ - 1)
    out += (jax.ShapeDtypeStruct((k, 128), F32), COUNTS)
    return _call(_mix_kernel, out, [acc, cnt, add], "mix")


def _totals(keep_ref, cnt_ref, refs):
    k = keep_ref.shape[0]
    total, c = keep_ref[...], cnt_ref[...]
    for r in refs:
        total = total + r[:k, :].astype(F32)
        c = c + _unpack_counts(r[k:, :])
    return total, c


def _far_kernel(keep_ref, cnt_ref, *refs):
    o_ref = refs[-1]
    k = keep_ref.shape[0]
    total, c = _totals(keep_ref, cnt_ref, refs[: NZ - 1])
    o_ref[:k, :] = total.astype(BF16)
    o_ref[k:, :] = _pack_counts(c)


def _final_kernel(id_ref, keep_ref, cnt_ref, *refs):
    other_ref, c_ref, o_ref = refs[-3:]
    k = c_ref.shape[0] // 2
    xh = _dp(id_ref) // NZ
    cols = pl.ds(pl.multiple_of(_dp(id_ref) * 128, 128), 128)
    mine = _totals(keep_ref, cnt_ref, refs[:-3])
    other = other_ref[:k, :].astype(F32), _unpack_counts(other_ref[k:, :])
    for side, (total, c) in ((xh, mine), (1 - xh, other)):
        off = pl.multiple_of(side * k, k)
        cnt = jnp.concatenate([c[q : q + 1, :] for q in range(k // 128)], axis=1)
        top = total + PRIOR * c_ref[pl.ds(off, k), cols].astype(F32)
        o_ref[:, pl.ds(off, k)] = top.T / (cnt + PRIOR)


def finish(ident, parts, other, centroids):
    return pl.pallas_call(
        _final_kernel,
        out_shape=jax.ShapeDtypeStruct((128, centroids.shape[0]), F32),
        in_specs=[SMEM] + [VMEM] * (len(parts) + 2),
        out_specs=VMEM,
        compiler_params=_params(12),
        name="finish",
    )(ident, *parts, other, centroids)


def _slots():
    place = {}
    for a in range(4):
        place[0, a] = (0, a * 128)
        place[2, a] = (3, a * 128)
        place[1, a] = (1 if a < 2 else 2, (a % 2) * 128)
        place[3, a] = (1 if a >= 2 else 2, 256 + (a % 2) * 128)
    return [place[b, a] for b in range(4) for a in range(4)]


def _gather_slots(refs, row):
    return jnp.concatenate(
        [refs[n][row : row + 1, off : off + 128] for n, off in _slots()], axis=0
    )


def _merge(pairs, gain):
    m = functools.reduce(jnp.maximum, [p[0] for p in pairs])
    s = sum(p[1] * jnp.exp2((p[0] - m) * gain) for p in pairs)
    return m, s


def _absolute(id_ref):
    dp, cent = _dp(id_ref), id_ref[0] % 16
    x, y, core = (dp // NZ) * 2 + cent // 8, (cent // 2) % NY, cent % 2
    first = jnp.where(core == 0, y, x)
    second = jnp.where(core == 0, x, y)
    return [((second - b) % 4) * 4 + (first - a) % 4 for b in range(4) for a in range(4)]


def _pack_kernel(gain, id_ref, *refs):
    stats, o_ref, t_ref = refs[:4], refs[-2], refs[-1]
    pairs = [(_gather_slots(stats, 2 * b), _gather_slots(stats, 2 * b + 1)) for b in range(2)]
    m, s = _merge(pairs, gain)
    for i, n in enumerate(_absolute(id_ref)):
        t_ref[0, pl.ds(n, 1), :] = m[i : i + 1, :]
        t_ref[1, pl.ds(n, 1), :] = s[i : i + 1, :]
    v = t_ref[...]
    for j in range(o_ref.shape[0]):
        o_ref[j] = v


def _scale_kernel(gain, id_ref, all_ref, *refs):
    stats, o_ref, t_ref = refs[:4], refs[-2], refs[-1]
    top, total = _merge([(all_ref[j, 0], all_ref[j, 1]) for j in range(all_ref.shape[0])], gain)
    t_ref[0], t_ref[1] = top, total
    order = _absolute(id_ref)
    top, total = [
        jnp.concatenate([t_ref[q, pl.ds(n, 1), :] for n in order], axis=0) for q in range(2)
    ]
    r = stats[0].shape[1]
    for b in range(2):
        q = jnp.exp2((_gather_slots(stats, 2 * b) - top) * gain) / total
        for i, (n, off) in enumerate(_slots()):
            o_ref[b : b + 1, n * r + off : n * r + off + 128] = q[i : i + 1, :]


def _statistics(kernel, shape, ident, args, name):
    return pl.pallas_call(
        kernel,
        out_shape=jax.ShapeDtypeStruct(shape, F32),
        in_specs=[SMEM] + [VMEM] * len(args),
        out_specs=VMEM,
        scratch_shapes=[pltpu.VMEM((2, 16, 128), F32)],
        compiler_params=_params(2),
        cost_estimate=LIGHT,
        name=name,
    )(ident, *args)


def _plane_groups():
    return [
        [(xh * 4 + z) * 16 + (xl * 4 + y) * 2 + core
         for xh in range(2) for xl in range(2) for y in range(NY)]
        for z in range(NZ) for core in range(2)
    ]


def local(points, centroids):
    features = points.shape[1]
    gain = BETA_GAIN * features ** (-0.5) * math.log2(math.e)
    ident = lax.axis_index(AXES).astype(jnp.int32).reshape(1)

    shards = [points] + [send_first(points, d) for d in (1, 2, 3)]
    shard, ident = lax.optimization_barrier((centroids, ident))
    whole = (centroids, send_core(shard))
    own, own_norm = load_half(ident, whole[0], 4)
    line_a, line_b = join(shards[0], shards[1], own_norm), join(shards[2], shards[3], own_norm)
    half = line_a.shape[0]
    up_a, down_b = send_second(line_a, 1), send_second(line_b, 3)
    sib, sib_norm = load_half(ident, whole[1], 4)
    cents = (own, sib)
    up_a, sib_norm = lax.optimization_barrier((up_a, sib_norm))
    far_a = send_second(up_a, 1)
    norms = (own_norm, sib_norm)
    up_b, down_a = send_second(line_b, 1), send_second(line_a, 3)

    ws, stats, xs = [], [], []

    def run(*xin):
        w, st, xp = score(ident, xin, cents, norms, gain, stats[-1:])
        ws.append(w)
        stats.append(st)
        xs.append(xp)

    run(line_a, line_b)
    down_b, stats[0] = lax.optimization_barrier((down_b, stats[0]))
    far_b = send_second(down_b, 3)
    run(up_a, down_b)
    run(up_b, down_a)
    run(far_a, far_b)

    shape = (NX * NY, 2, 16, 128)
    packs = _statistics(functools.partial(_pack_kernel, gain), shape, ident, stats, "stats_pack")
    packs = lax.all_to_all(packs, AXES, 0, 0, tiled=True, axis_index_groups=_plane_groups())
    shape = (8, sum(st.shape[1] for st in stats))
    scales = _statistics(
        functools.partial(_scale_kernel, gain), shape, ident, [packs] + stats, "stats_scale"
    )

    got, order = [], []
    for g in range(2):
        part = send_core(weighted_sums(1, g, ws, xs, scales, order))
        acc, cnt = weighted_sums(0, g, ws, xs, scales, order)
        *blocks, keep, cnt = mix(acc, cnt, part)
        order = [cnt]
        got.append([keep, cnt] + [send_z(v, d) for v, d in zip(blocks, SHIFTS)])
    rows = jax.ShapeDtypeStruct(blocks[0].shape, BF16)
    other = send_far(_call(_far_kernel, rows, got[0] + order, "far_sum"))
    return finish(ident, got[1], other, centroids)


def solution(mesh):
    return jax.shard_map(
        local,
        mesh=mesh,
        in_specs=(P(("dp", "cent"), None), P("cent", None)),
        out_specs=P("dp", "cent"),
        check_vma=False,
    )
```

```python
import functools
import math

import jax
import jax.numpy as jnp
from jax import lax
from jax.experimental import pallas as pl
from jax.experimental.pallas import tpu as pltpu
from jax.sharding import PartitionSpec as P

BETA_GAIN = 4.0
PRIOR = 0.5
F32 = jnp.float32
BF16 = jnp.bfloat16

NX, NY, NZ = 4, 4, 4
AXES = ("dp", "cent")
COUNT_ROWS = 32
LIGHT = pl.CostEstimate(flops=1024, bytes_accessed=1024, transcendentals=0)
COSTS = (pl.CostEstimate(flops=40 << 30, bytes_accessed=1024, transcendentals=0), LIGHT)
SHIFTS = (2, 1, 3, 0)
VMEM = pl.BlockSpec(memory_space=pltpu.VMEM)
SMEM = pl.BlockSpec(memory_space=pltpu.SMEM)


def _send(a, move):
    pairs = []
    for xh in range(2):
        for z in range(NZ):
            for xl in range(2):
                for y in range(NY):
                    for core in range(2):
                        src = (xh * 4 + z) * 16 + (xl * 4 + y) * 2 + core
                        x2, y2, z2, core2 = move(xh * 2 + xl, y, z, core)
                        x2, y2, z2 = x2 % NX, y2 % NY, z2 % NZ
                        dst = ((x2 // 2) * 4 + z2) * 16 + ((x2 % 2) * 4 + y2) * 2 + core2
                        pairs.append((src, dst))
    return lax.ppermute(a, AXES, pairs)


def send_first(a, d):
    return _send(a, lambda x, y, z, c: (x, y + d, z, c) if c == 0 else (x + d, y, z, c))


def send_second(a, d):
    return _send(a, lambda x, y, z, c: (x + d, y, z, c) if c == 0 else (x, y + d, z, c))


def send_core(a):
    return _send(a, lambda x, y, z, c: (x, y, z, 1 - c))


def send_z(a, d):
    return _send(a, lambda x, y, z, c: (x, y, z + d, c))


def send_far(a):
    return _send(a, lambda x, y, z, c: (x + 2, y, z, c))


def _params(mib):
    return pltpu.CompilerParams(vmem_limit_bytes=mib << 20)


def _load_kernel(id_ref, c_ref, half_ref, o_ref, sems):
    k = half_ref.shape[0]
    n = sems.shape[0]
    step = k // n
    base = (_dp(id_ref) // NZ) * k
    copies = []
    for j in range(n):
        src = c_ref.at[pl.ds(pl.multiple_of(base + j * step, step), step), :]
        dst = half_ref.at[pl.ds(j * step, step), :]
        copies.append(pltpu.make_async_copy(src, dst, sems.at[j]))
        copies[-1].start()
    for j in range(n):
        copies[j].wait()
        rows = slice(j * step, (j + 1) * step)
        v = half_ref[rows, :].astype(F32)
        s = 0.5 * jnp.sum(v * v, axis=1, keepdims=True)
        o_ref[rows, :] = jnp.broadcast_to(s, (step, 128))


def load_half(ident, cents, mib):
    k, d = cents.shape[0] // 2, cents.shape[1]
    return pl.pallas_call(
        _load_kernel,
        out_shape=(
            jax.ShapeDtypeStruct((k, d), BF16),
            jax.ShapeDtypeStruct((k, 128), F32),
        ),
        in_specs=[SMEM, pl.BlockSpec(memory_space=pltpu.HBM)],
        out_specs=(VMEM, VMEM),
        scratch_shapes=[pltpu.SemaphoreType.DMA((8,))],
        compiler_params=_params(mib),
        cost_estimate=LIGHT,
        name="load_half",
    )(ident, cents)


def _join_kernel(*refs):
    pos = 0
    for r in refs[:2]:
        n = r.shape[0]
        refs[-1][pos : pos + n, :] = r[...]
        pos += n


def join(a, b, *after):
    parts = (a, b, *after)
    rows, d = a.shape[0] + b.shape[0], a.shape[1]
    return pl.pallas_call(
        _join_kernel,
        out_shape=jax.ShapeDtypeStruct((rows, d), parts[0].dtype),
        in_specs=[VMEM] * len(parts),
        out_specs=VMEM,
        compiler_params=_params(2),
        name="join",
    )(*parts)


def _dp(id_ref):
    return id_ref[0] // 16


def _block(dp, n):
    xh = (dp // NZ + 1 - n // NZ) % 2
    return xh * NZ + (dp + SHIFTS[n % NZ]) % NZ


def _score_kernel(gain, n_x, id_ref, *refs):
    x_refs = refs[:n_x]
    c_refs, h_refs = refs[n_x : n_x + 2], refs[n_x + 2 : n_x + 4]
    w_ref, st_ref, xp_ref, u_ref, x_all_ref = refs[-5:]
    k = h_refs[0].shape[0]
    r = w_ref.shape[2]
    kb = 256
    pos = 0
    for x_ref in x_refs:
        n = x_ref.shape[0]
        x_all_ref[pos : pos + n, :] = x_ref[...]
        pos += n

    def dots(b, j):
        rows = slice(j * kb, (j + 1) * kb)
        u = lax.dot_general(
            c_refs[b][rows, :], x_all_ref[...], (((1,), (1,)), ((), ())), preferred_element_type=F32
        )
        u = u - jnp.tile(h_refs[b][rows, :], (1, r // 128))
        u_ref[b, rows, :] = u
        return jnp.max(u, axis=0, keepdims=True)

    def weights(b, j, m):
        rows = slice(j * kb, (j + 1) * kb)
        w = jnp.exp2((u_ref[b, rows, :] - m) * gain)
        w_ref[b, rows, :] = w.astype(BF16)
        return jnp.sum(w, axis=0, keepdims=True)

    def largest(ms):
        return functools.reduce(jnp.maximum, ms)

    nj = k // kb
    m0 = largest([dots(0, j) for j in range(nj)])
    ms, ss = [], []
    for j in range(nj):
        ms.append(dots(1, j))
        ss.append(weights(0, j, m0))
    m1 = largest(ms)
    st_ref[0:1, :] = m0
    st_ref[1:2, :] = sum(ss)
    for f in range(2 * NZ):
        off = pl.multiple_of(_block(_dp(id_ref), f) * 128, 128)
        pos = 0
        for x_ref in x_refs:
            n = x_ref.shape[0]
            xp_ref[pos : pos + n, f * 128 : (f + 1) * 128] = x_ref[:, pl.ds(off, 128)]
            pos += n
    st_ref[2:3, :] = m1
    st_ref[3:4, :] = sum([weights(1, j, m1) for j in range(nj)])
    st_ref[4:8, :] = jnp.zeros((4, r), F32)


def score(ident, xs, cents, norms, gain, after):
    r, d = sum(x.shape[0] for x in xs), xs[0].shape[1]
    k = norms[0].shape[0]
    return pl.pallas_call(
        functools.partial(_score_kernel, gain, len(xs)),
        out_shape=(
            jax.ShapeDtypeStruct((2, k, r), BF16),
            jax.ShapeDtypeStruct((8, r), F32),
            jax.ShapeDtypeStruct((r, d), BF16),
        ),
        in_specs=[SMEM] + [VMEM] * (len(xs) + 4 + len(after)),
        out_specs=(VMEM, VMEM, VMEM),
        scratch_shapes=[pltpu.VMEM((2, k, r), F32), pltpu.VMEM((r, d), BF16)],
        compiler_params=_params(14),
        cost_estimate=LIGHT,
        name="score",
    )(ident, *xs, *cents, *norms, *after)


def _sum_kernel(half, group, n_arr, *refs):
    w_refs, x_refs, sc_ref = refs[:n_arr], refs[n_arr : 2 * n_arr], refs[2 * n_arr]
    packed = half == 1
    out_ref, cnt_ref = refs[-2:]
    k = w_refs[0].shape[1]
    kb = 256
    per = kb // 128
    cols = slice(group * NZ * 128, (group + 1) * NZ * 128)
    for j in range(k // kb):
        rows = slice(j * kb, (j + 1) * kb)
        acc, lanes, pos = None, None, 0
        for a in range(n_arr):
            r = w_refs[a].shape[2]
            sc = sc_ref[half : half + 1, pos : pos + r]
            pos += r
            w = (w_refs[a][half, rows, :].astype(F32) * sc).astype(BF16)
            wf = w.astype(F32)
            for t in range(r // 128):
                part = wf[:, t * 128 : (t + 1) * 128]
                lanes = part if lanes is None else lanes + part
            d = jnp.dot(w, x_refs[a][:, cols], preferred_element_type=F32)
            acc = d if acc is None else acc + d
        col = jnp.sum(lanes.T, axis=0, keepdims=True)
        for t in range(per):
            cnt_ref[j * per + t : j * per + t + 1, :] = col[:, t * 128 : (t + 1) * 128]
        for f in range(NZ):
            out_ref[f, rows, :] = acc[:, f * 128 : (f + 1) * 128].astype(out_ref.dtype)
    if packed:
        for f in range(NZ):
            out_ref[f, k:, :] = _pack_counts(cnt_ref[...])


def _pack_counts(c):
    hi = c.astype(BF16).astype(F32)
    mid = (c - hi).astype(BF16).astype(F32)
    lo = (c - hi) - mid
    return jnp.concatenate([hi, mid, lo, jnp.zeros_like(lo)], axis=0).astype(BF16)


def _unpack_counts(rows):
    t = rows.astype(F32)
    return (t[0:8] + t[8:16]) + t[16:24]


COUNTS = jax.ShapeDtypeStruct((8, 128), F32)


def weighted_sums(half, group, ws, xs, scales, after=()):
    n_arr = len(ws)
    k, r = ws[0].shape[1:]
    operands = [*ws, *xs, scales, *after]
    if half == 1:
        out_shape = jax.ShapeDtypeStruct((NZ, k + COUNT_ROWS, 128), BF16)
        out_specs, scratch = VMEM, [pltpu.VMEM((8, 128), F32)]
    else:
        out_shape = (jax.ShapeDtypeStruct((NZ, k, 128), F32), COUNTS)
        out_specs, scratch = (VMEM, VMEM), []
    return pl.pallas_call(
        functools.partial(_sum_kernel, half, group, n_arr),
        out_shape=out_shape,
        in_specs=[VMEM] * len(operands),
        out_specs=out_specs,
        scratch_shapes=scratch,
        compiler_params=_params(14),
        cost_estimate=COSTS[half],
        name="sums_sib" if half else "sums_own",
    )(*operands)


def _call(kernel, out_shape, args, name, mib=8):
    many = isinstance(out_shape, tuple)
    return pl.pallas_call(
        kernel,
        out_shape=out_shape,
        in_specs=[VMEM] * len(args),
        out_specs=(VMEM,) * len(out_shape) if many else VMEM,
        compiler_params=_params(mib),
        cost_estimate=LIGHT,
        name=name,
    )(*args)


def _mix_kernel(acc_ref, cnt_ref, add_ref, *refs):
    keep_ref, sum_ref = refs[-2:]
    outs = refs[-2 - (NZ - 1) : -2]
    k = acc_ref.shape[1]
    c = cnt_ref[...] + _unpack_counts(add_ref[0, k:, :])
    sum_ref[...] = c
    packed = _pack_counts(c)
    for f in range(NZ - 1):
        outs[f][:k, :] = (acc_ref[f] + add_ref[f, :k, :].astype(F32)).astype(BF16)
        outs[f][k:, :] = packed
    keep_ref[...] = acc_ref[NZ - 1] + add_ref[NZ - 1, :k, :].astype(F32)


def mix(acc, cnt, add):
    k = acc.shape[1]
    out = (jax.ShapeDtypeStruct((k + COUNT_ROWS, 128), BF16),) * (NZ - 1)
    out += (jax.ShapeDtypeStruct((k, 128), F32), COUNTS)
    return _call(_mix_kernel, out, [acc, cnt, add], "mix")


def _totals(keep_ref, cnt_ref, refs):
    k = keep_ref.shape[0]
    total, c = keep_ref[...], cnt_ref[...]
    for r in refs:
        total = total + r[:k, :].astype(F32)
        c = c + _unpack_counts(r[k:, :])
    return total, c


def _far_kernel(keep_ref, cnt_ref, *refs):
    o_ref = refs[-1]
    k = keep_ref.shape[0]
    total, c = _totals(keep_ref, cnt_ref, refs[: NZ - 1])
    o_ref[:k, :] = total.astype(BF16)
    o_ref[k:, :] = _pack_counts(c)


def _final_kernel(id_ref, keep_ref, cnt_ref, *refs):
    other_ref, c_ref, o_ref = refs[-3:]
    k = c_ref.shape[0] // 2
    xh = _dp(id_ref) // NZ
    cols = pl.ds(pl.multiple_of(_dp(id_ref) * 128, 128), 128)
    mine = _totals(keep_ref, cnt_ref, refs[:-3])
    other = other_ref[:k, :].astype(F32), _unpack_counts(other_ref[k:, :])
    for side, (total, c) in ((xh, mine), (1 - xh, other)):
        off = pl.multiple_of(side * k, k)
        cnt = jnp.concatenate([c[q : q + 1, :] for q in range(k // 128)], axis=1)
        top = total + PRIOR * c_ref[pl.ds(off, k), cols].astype(F32)
        o_ref[:, pl.ds(off, k)] = top.T / (cnt + PRIOR)


def finish(ident, parts, other, centroids):
    return pl.pallas_call(
        _final_kernel,
        out_shape=jax.ShapeDtypeStruct((128, centroids.shape[0]), F32),
        in_specs=[SMEM] + [VMEM] * (len(parts) + 2),
        out_specs=VMEM,
        compiler_params=_params(12),
        name="finish",
    )(ident, *parts, other, centroids)


def _slots():
    place = {}
    for a in range(4):
        place[0, a] = (0, a * 128)
        place[2, a] = (3 + a // 2, (a % 2) * 128)
        place[1, a] = (1 if a < 2 else 2, (a % 2) * 128)
        place[3, a] = (1 if a >= 2 else 2, 256 + (a % 2) * 128)
    return [place[b, a] for b in range(4) for a in range(4)]


def _gather_slots(refs, row):
    return jnp.concatenate(
        [refs[n][row : row + 1, off : off + 128] for n, off in _slots()], axis=0
    )


def _merge(pairs, gain):
    m = functools.reduce(jnp.maximum, [p[0] for p in pairs])
    s = sum(p[1] * jnp.exp2((p[0] - m) * gain) for p in pairs)
    return m, s


def _absolute(id_ref):
    dp, cent = _dp(id_ref), id_ref[0] % 16
    x, y, core = (dp // NZ) * 2 + cent // 8, (cent // 2) % NY, cent % 2
    first = jnp.where(core == 0, y, x)
    second = jnp.where(core == 0, x, y)
    return [((second - b) % 4) * 4 + (first - a) % 4 for b in range(4) for a in range(4)]


def _pack_kernel(gain, id_ref, *refs):
    stats, o_ref, t_ref = refs[:-2], refs[-2], refs[-1]
    pairs = [(_gather_slots(stats, 2 * b), _gather_slots(stats, 2 * b + 1)) for b in range(2)]
    m, s = _merge(pairs, gain)
    for i, n in enumerate(_absolute(id_ref)):
        t_ref[0, pl.ds(n, 1), :] = m[i : i + 1, :]
        t_ref[1, pl.ds(n, 1), :] = s[i : i + 1, :]
    v = t_ref[...]
    for j in range(o_ref.shape[0]):
        o_ref[j] = v


def _scale_kernel(gain, id_ref, all_ref, *refs):
    stats, o_ref, t_ref = refs[:-2], refs[-2], refs[-1]
    top, total = _merge([(all_ref[j, 0], all_ref[j, 1]) for j in range(all_ref.shape[0])], gain)
    t_ref[0], t_ref[1] = top, total
    order = _absolute(id_ref)
    top, total = [
        jnp.concatenate([t_ref[q, pl.ds(n, 1), :] for n in order], axis=0) for q in range(2)
    ]
    base = [sum(st.shape[1] for st in stats[:n]) for n in range(len(stats))]
    for b in range(2):
        q = jnp.exp2((_gather_slots(stats, 2 * b) - top) * gain) / total
        for i, (n, off) in enumerate(_slots()):
            lane = base[n] + off
            o_ref[b : b + 1, lane : lane + 128] = q[i : i + 1, :]


def _statistics(kernel, shape, ident, args, name):
    return pl.pallas_call(
        kernel,
        out_shape=jax.ShapeDtypeStruct(shape, F32),
        in_specs=[SMEM] + [VMEM] * len(args),
        out_specs=VMEM,
        scratch_shapes=[pltpu.VMEM((2, 16, 128), F32)],
        compiler_params=_params(2),
        cost_estimate=LIGHT,
        name=name,
    )(ident, *args)


def _plane_groups():
    return [
        [(xh * 4 + z) * 16 + (xl * 4 + y) * 2 + core
         for xh in range(2) for xl in range(2) for y in range(NY)]
        for z in range(NZ) for core in range(2)
    ]


def local(points, centroids):
    features = points.shape[1]
    gain = BETA_GAIN * features ** (-0.5) * math.log2(math.e)
    ident = lax.axis_index(AXES).astype(jnp.int32).reshape(1)

    shards = [points] + [send_first(points, d) for d in (1, 2, 3)]
    shard, ident = lax.optimization_barrier((centroids, ident))
    whole = (centroids, send_core(shard))
    own, own_norm = load_half(ident, whole[0], 4)
    line_a, line_b = join(shards[0], shards[1], own_norm), join(shards[2], shards[3], own_norm)
    half = line_a.shape[0]
    up_a, down_b = send_second(line_a, 1), send_second(line_b, 3)
    sib, sib_norm = load_half(ident, whole[1], 4)
    cents = (own, sib)
    up_a, sib_norm = lax.optimization_barrier((up_a, sib_norm))
    far_a = send_second(up_a, 1)
    norms = (own_norm, sib_norm)
    up_b, down_a = send_second(line_b, 1), send_second(line_a, 3)

    ws, stats, xs = [], [], []

    def run(*xin):
        w, st, xp = score(ident, xin, cents, norms, gain, stats[-1:])
        ws.append(w)
        stats.append(st)
        xs.append(xp)

    run(line_a, line_b)
    down_b, stats[0] = lax.optimization_barrier((down_b, stats[0]))
    far_b = send_second(down_b, 3)
    run(up_a, down_b)
    run(up_b, down_a)
    run(far_a)
    run(far_b)

    shape = (NX * NY, 2, 16, 128)
    packs = _statistics(functools.partial(_pack_kernel, gain), shape, ident, stats, "stats_pack")
    packs = lax.all_to_all(packs, AXES, 0, 0, tiled=True, axis_index_groups=_plane_groups())
    shape = (8, sum(st.shape[1] for st in stats))
    scales = _statistics(
        functools.partial(_scale_kernel, gain), shape, ident, [packs] + stats, "stats_scale"
    )

    got, order = [], []
    for g in range(2):
        part = send_core(weighted_sums(1, g, ws, xs, scales, order))
        acc, cnt = weighted_sums(0, g, ws, xs, scales, order)
        *blocks, keep, cnt = mix(acc, cnt, part)
        order = [cnt]
        got.append([keep, cnt] + [send_z(v, d) for v, d in zip(blocks, SHIFTS)])
    rows = jax.ShapeDtypeStruct(blocks[0].shape, BF16)
    other = send_far(_call(_far_kernel, rows, got[0] + order, "far_sum"))
    return finish(ident, got[1], other, centroids)


def solution(mesh):
    return jax.shard_map(
        local,
        mesh=mesh,
        in_specs=(P(("dp", "cent"), None), P("cent", None)),
        out_specs=P("dp", "cent"),
        check_vma=False,
    )
```

```python
import functools
import math

import jax
import jax.numpy as jnp
from jax import lax
from jax.experimental import pallas as pl
from jax.experimental.pallas import tpu as pltpu
from jax.sharding import PartitionSpec as P

BETA_GAIN = 4.0
PRIOR = 0.5
F32 = jnp.float32
BF16 = jnp.bfloat16

NX, NY, NZ = 4, 4, 4
AXES = ("dp", "cent")
COUNT_ROWS = 32
LIGHT = pl.CostEstimate(flops=1024, bytes_accessed=1024, transcendentals=0)
COSTS = (pl.CostEstimate(flops=40 << 30, bytes_accessed=1024, transcendentals=0), LIGHT)
SHIFTS = (2, 1, 3, 0)
VMEM = pl.BlockSpec(memory_space=pltpu.VMEM)
SMEM = pl.BlockSpec(memory_space=pltpu.SMEM)


def _send(a, move):
    pairs = []
    for xh in range(2):
        for z in range(NZ):
            for xl in range(2):
                for y in range(NY):
                    for core in range(2):
                        src = (xh * 4 + z) * 16 + (xl * 4 + y) * 2 + core
                        x2, y2, z2, core2 = move(xh * 2 + xl, y, z, core)
                        x2, y2, z2 = x2 % NX, y2 % NY, z2 % NZ
                        dst = ((x2 // 2) * 4 + z2) * 16 + ((x2 % 2) * 4 + y2) * 2 + core2
                        pairs.append((src, dst))
    return lax.ppermute(a, AXES, pairs)


def send_first(a, d):
    return _send(a, lambda x, y, z, c: (x, y + d, z, c) if c == 0 else (x + d, y, z, c))


def send_second(a, d):
    return _send(a, lambda x, y, z, c: (x + d, y, z, c) if c == 0 else (x, y + d, z, c))


def send_core(a):
    return _send(a, lambda x, y, z, c: (x, y, z, 1 - c))


def send_z(a, d):
    return _send(a, lambda x, y, z, c: (x, y, z + d, c))


def send_far(a):
    return _send(a, lambda x, y, z, c: (x + 2, y, z, c))


def _params(mib):
    return pltpu.CompilerParams(vmem_limit_bytes=mib << 20)


def _load_kernel(gain, id_ref, c_ref, half_ref, o_ref, sems):
    k = half_ref.shape[0]
    n = sems.shape[0]
    step = k // n
    base = (_dp(id_ref) // NZ) * k
    copies = []
    for j in range(n):
        src = c_ref.at[pl.ds(pl.multiple_of(base + j * step, step), step), :]
        dst = half_ref.at[pl.ds(j * step, step), :]
        copies.append(pltpu.make_async_copy(src, dst, sems.at[j]))
        copies[-1].start()
    for j in range(n):
        copies[j].wait()
        rows = slice(j * step, (j + 1) * step)
        v = half_ref[rows, :].astype(F32)
        s = (0.5 * gain) * jnp.sum(v * v, axis=1, keepdims=True)
        o_ref[rows, :] = jnp.broadcast_to(s, (step, 128))


def load_half(ident, cents, mib, gain):
    k, d = cents.shape[0] // 2, cents.shape[1]
    return pl.pallas_call(
        functools.partial(_load_kernel, gain),
        out_shape=(
            jax.ShapeDtypeStruct((k, d), BF16),
            jax.ShapeDtypeStruct((k, 128), F32),
        ),
        in_specs=[SMEM, pl.BlockSpec(memory_space=pltpu.HBM)],
        out_specs=(VMEM, VMEM),
        scratch_shapes=[pltpu.SemaphoreType.DMA((8,))],
        compiler_params=_params(mib),
        cost_estimate=LIGHT,
        name="load_half",
    )(ident, cents)


def _join_kernel(*refs):
    pos = 0
    for r in refs[:2]:
        n = r.shape[0]
        refs[-1][pos : pos + n, :] = r[...]
        pos += n


def join(a, b, *after):
    parts = (a, b, *after)
    rows, d = a.shape[0] + b.shape[0], a.shape[1]
    return pl.pallas_call(
        _join_kernel,
        out_shape=jax.ShapeDtypeStruct((rows, d), parts[0].dtype),
        in_specs=[VMEM] * len(parts),
        out_specs=VMEM,
        compiler_params=_params(2),
        name="join",
    )(*parts)


def _dp(id_ref):
    return id_ref[0] // 16


def _block(dp, n):
    xh = (dp // NZ + 1 - n // NZ) % 2
    return xh * NZ + (dp + SHIFTS[n % NZ]) % NZ


def _score_kernel(gain, n_x, id_ref, *refs):
    x_refs = refs[:n_x]
    c_refs, h_refs = refs[n_x : n_x + 2], refs[n_x + 2 : n_x + 4]
    w_ref, st_ref, xp_ref, u_ref, x_all_ref = refs[-5:]
    k = h_refs[0].shape[0]
    r = w_ref.shape[2]
    kb = 256
    pos = 0
    for x_ref in x_refs:
        n = x_ref.shape[0]
        x_all_ref[pos : pos + n, :] = x_ref[...]
        pos += n

    def dots(b, j):
        rows = slice(j * kb, (j + 1) * kb)
        u = lax.dot_general(
            c_refs[b][rows, :], x_all_ref[...], (((1,), (1,)), ((), ())), preferred_element_type=F32
        )
        u = u * gain - jnp.tile(h_refs[b][rows, :], (1, r // 128))
        u_ref[b, rows, :] = u
        return jnp.max(u, axis=0, keepdims=True)

    def weights(b, j, m):
        rows = slice(j * kb, (j + 1) * kb)
        w = jnp.exp2(u_ref[b, rows, :] - m)
        w_ref[b, rows, :] = w.astype(BF16)
        return jnp.sum(w, axis=0, keepdims=True)

    def largest(ms):
        return functools.reduce(jnp.maximum, ms)

    nj = k // kb
    m0 = largest([dots(0, j) for j in range(nj)])
    ms, ss = [], []
    for j in range(nj):
        ms.append(dots(1, j))
        ss.append(weights(0, j, m0))
    m1 = largest(ms)
    st_ref[0:1, :] = m0
    st_ref[1:2, :] = sum(ss)
    for f in range(2 * NZ):
        off = pl.multiple_of(_block(_dp(id_ref), f) * 128, 128)
        pos = 0
        for x_ref in x_refs:
            n = x_ref.shape[0]
            xp_ref[pos : pos + n, f * 128 : (f + 1) * 128] = x_ref[:, pl.ds(off, 128)]
            pos += n
    st_ref[2:3, :] = m1
    st_ref[3:4, :] = sum([weights(1, j, m1) for j in range(nj)])
    st_ref[4:8, :] = jnp.zeros((4, r), F32)


def score(ident, xs, cents, norms, gain, after):
    r, d = sum(x.shape[0] for x in xs), xs[0].shape[1]
    k = norms[0].shape[0]
    return pl.pallas_call(
        functools.partial(_score_kernel, gain, len(xs)),
        out_shape=(
            jax.ShapeDtypeStruct((2, k, r), BF16),
            jax.ShapeDtypeStruct((8, r), F32),
            jax.ShapeDtypeStruct((r, d), BF16),
        ),
        in_specs=[SMEM] + [VMEM] * (len(xs) + 4 + len(after)),
        out_specs=(VMEM, VMEM, VMEM),
        scratch_shapes=[pltpu.VMEM((2, k, r), F32), pltpu.VMEM((r, d), BF16)],
        compiler_params=_params(14),
        cost_estimate=LIGHT,
        name="score",
    )(ident, *xs, *cents, *norms, *after)


def _sum_kernel(half, group, n_arr, *refs):
    w_refs, x_refs, sc_ref = refs[:n_arr], refs[n_arr : 2 * n_arr], refs[2 * n_arr]
    packed = half == 1
    out_ref, cnt_ref = refs[-2:]
    k = w_refs[0].shape[1]
    kb = 256
    per = kb // 128
    cols = slice(group * NZ * 128, (group + 1) * NZ * 128)
    for j in range(k // kb):
        rows = slice(j * kb, (j + 1) * kb)
        acc, lanes, pos = None, None, 0
        for a in range(n_arr):
            r = w_refs[a].shape[2]
            sc = sc_ref[half : half + 1, pos : pos + r]
            pos += r
            w = (w_refs[a][half, rows, :].astype(F32) * sc).astype(BF16)
            wf = w.astype(F32)
            for t in range(r // 128):
                part = wf[:, t * 128 : (t + 1) * 128]
                lanes = part if lanes is None else lanes + part
            d = jnp.dot(w, x_refs[a][:, cols], preferred_element_type=F32)
            acc = d if acc is None else acc + d
        col = jnp.sum(lanes.T, axis=0, keepdims=True)
        for t in range(per):
            cnt_ref[j * per + t : j * per + t + 1, :] = col[:, t * 128 : (t + 1) * 128]
        for f in range(NZ):
            out_ref[f, rows, :] = acc[:, f * 128 : (f + 1) * 128].astype(out_ref.dtype)
    if packed:
        for f in range(NZ):
            out_ref[f, k:, :] = _pack_counts(cnt_ref[...])


def _pack_counts(c):
    hi = c.astype(BF16).astype(F32)
    mid = (c - hi).astype(BF16).astype(F32)
    lo = (c - hi) - mid
    return jnp.concatenate([hi, mid, lo, jnp.zeros_like(lo)], axis=0).astype(BF16)


def _unpack_counts(rows):
    t = rows.astype(F32)
    return (t[0:8] + t[8:16]) + t[16:24]


COUNTS = jax.ShapeDtypeStruct((8, 128), F32)


def weighted_sums(half, group, ws, xs, scales, after=()):
    n_arr = len(ws)
    k, r = ws[0].shape[1:]
    operands = [*ws, *xs, scales, *after]
    if half == 1:
        out_shape = jax.ShapeDtypeStruct((NZ, k + COUNT_ROWS, 128), BF16)
        out_specs, scratch = VMEM, [pltpu.VMEM((8, 128), F32)]
    else:
        out_shape = (jax.ShapeDtypeStruct((NZ, k, 128), F32), COUNTS)
        out_specs, scratch = (VMEM, VMEM), []
    return pl.pallas_call(
        functools.partial(_sum_kernel, half, group, n_arr),
        out_shape=out_shape,
        in_specs=[VMEM] * len(operands),
        out_specs=out_specs,
        scratch_shapes=scratch,
        compiler_params=_params(14),
        cost_estimate=COSTS[half],
        name="sums_sib" if half else "sums_own",
    )(*operands)


def _call(kernel, out_shape, args, name, mib=8):
    many = isinstance(out_shape, tuple)
    return pl.pallas_call(
        kernel,
        out_shape=out_shape,
        in_specs=[VMEM] * len(args),
        out_specs=(VMEM,) * len(out_shape) if many else VMEM,
        compiler_params=_params(mib),
        cost_estimate=LIGHT,
        name=name,
    )(*args)


def _mix_kernel(acc_ref, cnt_ref, add_ref, *refs):
    keep_ref, sum_ref = refs[-2:]
    outs = refs[-2 - (NZ - 1) : -2]
    k = acc_ref.shape[1]
    c = cnt_ref[...] + _unpack_counts(add_ref[0, k:, :])
    sum_ref[...] = c
    packed = _pack_counts(c)
    for f in range(NZ - 1):
        outs[f][:k, :] = (acc_ref[f] + add_ref[f, :k, :].astype(F32)).astype(BF16)
        outs[f][k:, :] = packed
    keep_ref[...] = acc_ref[NZ - 1] + add_ref[NZ - 1, :k, :].astype(F32)


def mix(acc, cnt, add):
    k = acc.shape[1]
    out = (jax.ShapeDtypeStruct((k + COUNT_ROWS, 128), BF16),) * (NZ - 1)
    out += (jax.ShapeDtypeStruct((k, 128), F32), COUNTS)
    return _call(_mix_kernel, out, [acc, cnt, add], "mix")


def _totals(keep_ref, cnt_ref, refs):
    k = keep_ref.shape[0]
    total, c = keep_ref[...], cnt_ref[...]
    for r in refs:
        total = total + r[:k, :].astype(F32)
        c = c + _unpack_counts(r[k:, :])
    return total, c


def _far_kernel(keep_ref, cnt_ref, *refs):
    o_ref = refs[-1]
    k = keep_ref.shape[0]
    total, c = _totals(keep_ref, cnt_ref, refs[: NZ - 1])
    o_ref[:k, :] = total.astype(BF16)
    o_ref[k:, :] = _pack_counts(c)


def _final_kernel(id_ref, keep_ref, cnt_ref, *refs):
    other_ref, c_ref, o_ref = refs[-3:]
    k = c_ref.shape[0] // 2
    xh = _dp(id_ref) // NZ
    cols = pl.ds(pl.multiple_of(_dp(id_ref) * 128, 128), 128)
    mine = _totals(keep_ref, cnt_ref, refs[:-3])
    other = other_ref[:k, :].astype(F32), _unpack_counts(other_ref[k:, :])
    for side, (total, c) in ((xh, mine), (1 - xh, other)):
        off = pl.multiple_of(side * k, k)
        cnt = jnp.concatenate([c[q : q + 1, :] for q in range(k // 128)], axis=1)
        top = total + PRIOR * c_ref[pl.ds(off, k), cols].astype(F32)
        o_ref[:, pl.ds(off, k)] = top.T / (cnt + PRIOR)


def finish(ident, parts, other, centroids):
    return pl.pallas_call(
        _final_kernel,
        out_shape=jax.ShapeDtypeStruct((128, centroids.shape[0]), F32),
        in_specs=[SMEM] + [VMEM] * (len(parts) + 2),
        out_specs=VMEM,
        compiler_params=_params(12),
        name="finish",
    )(ident, *parts, other, centroids)


def _slots():
    place = {}
    for a in range(4):
        place[0, a] = (0, a * 128)
        place[2, a] = (3 + a // 2, (a % 2) * 128)
        place[1, a] = (1 if a < 2 else 2, (a % 2) * 128)
        place[3, a] = (1 if a >= 2 else 2, 256 + (a % 2) * 128)
    return [place[b, a] for b in range(4) for a in range(4)]


def _gather_slots(refs, row):
    return jnp.concatenate(
        [refs[n][row : row + 1, off : off + 128] for n, off in _slots()], axis=0
    )


def _merge(pairs, gain):
    m = functools.reduce(jnp.maximum, [p[0] for p in pairs])
    s = sum(p[1] * jnp.exp2(p[0] - m) for p in pairs)
    return m, s


def _absolute(id_ref):
    dp, cent = _dp(id_ref), id_ref[0] % 16
    x, y, core = (dp // NZ) * 2 + cent // 8, (cent // 2) % NY, cent % 2
    first = jnp.where(core == 0, y, x)
    second = jnp.where(core == 0, x, y)
    return [((second - b) % 4) * 4 + (first - a) % 4 for b in range(4) for a in range(4)]


def _pack_kernel(gain, id_ref, *refs):
    stats, o_ref, t_ref = refs[:-2], refs[-2], refs[-1]
    pairs = [(_gather_slots(stats, 2 * b), _gather_slots(stats, 2 * b + 1)) for b in range(2)]
    m, s = _merge(pairs, gain)
    for i, n in enumerate(_absolute(id_ref)):
        t_ref[0, pl.ds(n, 1), :] = m[i : i + 1, :]
        t_ref[1, pl.ds(n, 1), :] = s[i : i + 1, :]
    v = t_ref[...]
    for j in range(o_ref.shape[0]):
        o_ref[j] = v


def _scale_kernel(gain, id_ref, all_ref, *refs):
    stats, o_ref, t_ref = refs[:-2], refs[-2], refs[-1]
    top, total = _merge([(all_ref[j, 0], all_ref[j, 1]) for j in range(all_ref.shape[0])], gain)
    t_ref[0], t_ref[1] = top, total
    order = _absolute(id_ref)
    top, total = [
        jnp.concatenate([t_ref[q, pl.ds(n, 1), :] for n in order], axis=0) for q in range(2)
    ]
    base = [sum(st.shape[1] for st in stats[:n]) for n in range(len(stats))]
    for b in range(2):
        q = jnp.exp2(_gather_slots(stats, 2 * b) - top) / total
        for i, (n, off) in enumerate(_slots()):
            lane = base[n] + off
            o_ref[b : b + 1, lane : lane + 128] = q[i : i + 1, :]


def _statistics(kernel, shape, ident, args, name):
    return pl.pallas_call(
        kernel,
        out_shape=jax.ShapeDtypeStruct(shape, F32),
        in_specs=[SMEM] + [VMEM] * len(args),
        out_specs=VMEM,
        scratch_shapes=[pltpu.VMEM((2, 16, 128), F32)],
        compiler_params=_params(2),
        cost_estimate=LIGHT,
        name=name,
    )(ident, *args)


def _plane_groups():
    return [
        [(xh * 4 + z) * 16 + (xl * 4 + y) * 2 + core
         for xh in range(2) for xl in range(2) for y in range(NY)]
        for z in range(NZ) for core in range(2)
    ]


def local(points, centroids):
    features = points.shape[1]
    gain = BETA_GAIN * features ** (-0.5) * math.log2(math.e)
    ident = lax.axis_index(AXES).astype(jnp.int32).reshape(1)

    shards = [points] + [send_first(points, d) for d in (1, 2, 3)]
    shard, ident = lax.optimization_barrier((centroids, ident))
    whole = (centroids, send_core(shard))
    own, own_norm = load_half(ident, whole[0], 4, gain)
    line_a, line_b = join(shards[0], shards[1], own_norm), join(shards[2], shards[3], own_norm)
    half = line_a.shape[0]
    up_a, down_b = send_second(line_a, 1), send_second(line_b, 3)
    sib, sib_norm = load_half(ident, whole[1], 4, gain)
    cents = (own, sib)
    up_a, sib_norm = lax.optimization_barrier((up_a, sib_norm))
    far_a = send_second(up_a, 1)
    norms = (own_norm, sib_norm)
    up_b, down_a = send_second(line_b, 1), send_second(line_a, 3)

    ws, stats, xs = [], [], []

    def run(*xin):
        w, st, xp = score(ident, xin, cents, norms, gain, stats[-1:])
        ws.append(w)
        stats.append(st)
        xs.append(xp)

    run(line_a, line_b)
    down_b, stats[0] = lax.optimization_barrier((down_b, stats[0]))
    far_b = send_second(down_b, 3)
    run(up_a, down_b)
    run(up_b, down_a)
    run(far_a)
    run(far_b)

    shape = (NX * NY, 2, 16, 128)
    packs = _statistics(functools.partial(_pack_kernel, gain), shape, ident, stats, "stats_pack")
    packs = lax.all_to_all(packs, AXES, 0, 0, tiled=True, axis_index_groups=_plane_groups())
    shape = (8, sum(st.shape[1] for st in stats))
    scales = _statistics(
        functools.partial(_scale_kernel, gain), shape, ident, [packs] + stats, "stats_scale"
    )

    got, order = [], []
    for g in range(2):
        part = send_core(weighted_sums(1, g, ws, xs, scales, order))
        acc, cnt = weighted_sums(0, g, ws, xs, scales, order)
        *blocks, keep, cnt = mix(acc, cnt, part)
        order = [cnt]
        got.append([keep, cnt] + [send_z(v, d) for v, d in zip(blocks, SHIFTS)])
    rows = jax.ShapeDtypeStruct(blocks[0].shape, BF16)
    other = send_far(_call(_far_kernel, rows, got[0] + order, "far_sum"))
    return finish(ident, got[1], other, centroids)


def solution(mesh):
    return jax.shard_map(
        local,
        mesh=mesh,
        in_specs=(P(("dp", "cent"), None), P("cent", None)),
        out_specs=P("dp", "cent"),
        check_vma=False,
    )
```

```python
import functools
import math

import jax
import jax.numpy as jnp
from jax import lax
from jax.experimental import pallas as pl
from jax.experimental.pallas import tpu as pltpu
from jax.sharding import PartitionSpec as P

BETA_GAIN = 4.0
PRIOR = 0.5
F32 = jnp.float32
BF16 = jnp.bfloat16

NX, NY, NZ = 4, 4, 4
AXES = ("dp", "cent")
COUNT_ROWS = 32
LIGHT = pl.CostEstimate(flops=1024, bytes_accessed=1024, transcendentals=0)
COSTS = (pl.CostEstimate(flops=40 << 30, bytes_accessed=1024, transcendentals=0), LIGHT)
SHIFTS = (2, 1, 3, 0)
VMEM = pl.BlockSpec(memory_space=pltpu.VMEM)
SMEM = pl.BlockSpec(memory_space=pltpu.SMEM)


def _send(a, move):
    pairs = []
    for xh in range(2):
        for z in range(NZ):
            for xl in range(2):
                for y in range(NY):
                    for core in range(2):
                        src = (xh * 4 + z) * 16 + (xl * 4 + y) * 2 + core
                        x2, y2, z2, core2 = move(xh * 2 + xl, y, z, core)
                        x2, y2, z2 = x2 % NX, y2 % NY, z2 % NZ
                        dst = ((x2 // 2) * 4 + z2) * 16 + ((x2 % 2) * 4 + y2) * 2 + core2
                        pairs.append((src, dst))
    return lax.ppermute(a, AXES, pairs)


def send_first(a, d):
    return _send(a, lambda x, y, z, c: (x, y + d, z, c) if c == 0 else (x + d, y, z, c))


def send_second(a, d):
    return _send(a, lambda x, y, z, c: (x + d, y, z, c) if c == 0 else (x, y + d, z, c))


def send_core(a):
    return _send(a, lambda x, y, z, c: (x, y, z, 1 - c))


def send_z(a, d):
    return _send(a, lambda x, y, z, c: (x, y, z + d, c))


def send_far(a):
    return _send(a, lambda x, y, z, c: (x + 2, y, z, c))


def _params(mib):
    return pltpu.CompilerParams(vmem_limit_bytes=mib << 20)


def _load_kernel(gain, id_ref, c_ref, half_ref, o_ref, sems):
    k = half_ref.shape[0]
    n = sems.shape[0]
    step = k // n
    base = (_dp(id_ref) // NZ) * k
    copies = []
    for j in range(n):
        src = c_ref.at[pl.ds(pl.multiple_of(base + j * step, step), step), :]
        dst = half_ref.at[pl.ds(j * step, step), :]
        copies.append(pltpu.make_async_copy(src, dst, sems.at[j]))
        copies[-1].start()
    for j in range(n):
        copies[j].wait()
        rows = slice(j * step, (j + 1) * step)
        v = half_ref[rows, :].astype(F32)
        s = (0.5 * gain) * jnp.sum(v * v, axis=1, keepdims=True)
        o_ref[rows, :] = jnp.broadcast_to(s, (step, 128))


def load_half(ident, cents, mib, gain):
    k, d = cents.shape[0] // 2, cents.shape[1]
    return pl.pallas_call(
        functools.partial(_load_kernel, gain),
        out_shape=(
            jax.ShapeDtypeStruct((k, d), BF16),
            jax.ShapeDtypeStruct((k, 128), F32),
        ),
        in_specs=[SMEM, pl.BlockSpec(memory_space=pltpu.HBM)],
        out_specs=(VMEM, VMEM),
        scratch_shapes=[pltpu.SemaphoreType.DMA((8,))],
        compiler_params=_params(mib),
        cost_estimate=LIGHT,
        name="load_half",
    )(ident, cents)


def _join_kernel(*refs):
    pos = 0
    for r in refs[:2]:
        n = r.shape[0]
        refs[-1][pos : pos + n, :] = r[...]
        pos += n


def join(a, b, *after):
    parts = (a, b, *after)
    rows, d = a.shape[0] + b.shape[0], a.shape[1]
    return pl.pallas_call(
        _join_kernel,
        out_shape=jax.ShapeDtypeStruct((rows, d), parts[0].dtype),
        in_specs=[VMEM] * len(parts),
        out_specs=VMEM,
        compiler_params=_params(2),
        name="join",
    )(*parts)


def _dp(id_ref):
    return id_ref[0] // 16


def _block(dp, n):
    xh = (dp // NZ + 1 - n // NZ) % 2
    return xh * NZ + (dp + SHIFTS[n % NZ]) % NZ


def _score_kernel(gain, n_x, id_ref, *refs):
    x_refs = refs[:n_x]
    c_refs, h_refs = refs[n_x : n_x + 2], refs[n_x + 2 : n_x + 4]
    w_ref, st_ref, xp_ref, u_ref, x_all_ref = refs[-5:]
    k = h_refs[0].shape[0]
    r = w_ref.shape[2]
    kb = 256
    pos = 0
    for x_ref in x_refs:
        n = x_ref.shape[0]
        x_all_ref[pos : pos + n, :] = x_ref[...]
        pos += n

    def dots(b, j):
        rows = slice(j * kb, (j + 1) * kb)
        u = lax.dot_general(
            c_refs[b][rows, :], x_all_ref[...], (((1,), (1,)), ((), ())), preferred_element_type=F32
        )
        u = u * gain - jnp.tile(h_refs[b][rows, :], (1, r // 128))
        u_ref[b, rows, :] = u
        return jnp.max(u, axis=0, keepdims=True)

    def weights(b, j, m):
        rows = slice(j * kb, (j + 1) * kb)
        w = jnp.exp2(u_ref[b, rows, :] - m)
        w_ref[b, rows, :] = w.astype(BF16)
        return jnp.sum(w, axis=0, keepdims=True)

    def largest(ms):
        return functools.reduce(jnp.maximum, ms)

    nj = k // kb
    m0 = largest([dots(0, j) for j in range(nj)])
    ms, ss = [], []
    for j in range(nj):
        ms.append(dots(1, j))
        ss.append(weights(0, j, m0))
    m1 = largest(ms)
    st_ref[0:1, :] = m0
    st_ref[1:2, :] = sum(ss)
    for f in range(2 * NZ):
        off = pl.multiple_of(_block(_dp(id_ref), f) * 128, 128)
        pos = 0
        for x_ref in x_refs:
            n = x_ref.shape[0]
            xp_ref[pos : pos + n, f * 128 : (f + 1) * 128] = x_ref[:, pl.ds(off, 128)]
            pos += n
    st_ref[2:3, :] = m1
    st_ref[3:4, :] = sum([weights(1, j, m1) for j in range(nj)])
    st_ref[4:8, :] = jnp.zeros((4, r), F32)


def score(ident, xs, cents, norms, gain, after):
    r, d = sum(x.shape[0] for x in xs), xs[0].shape[1]
    k = norms[0].shape[0]
    return pl.pallas_call(
        functools.partial(_score_kernel, gain, len(xs)),
        out_shape=(
            jax.ShapeDtypeStruct((2, k, r), BF16),
            jax.ShapeDtypeStruct((8, r), F32),
            jax.ShapeDtypeStruct((r, d), BF16),
        ),
        in_specs=[SMEM] + [VMEM] * (len(xs) + 4 + len(after)),
        out_specs=(VMEM, VMEM, VMEM),
        scratch_shapes=[pltpu.VMEM((2, k, r), F32), pltpu.VMEM((r, d), BF16)],
        compiler_params=_params(14),
        cost_estimate=LIGHT,
        name="score",
    )(ident, *xs, *cents, *norms, *after)


def _sum_kernel(half, group, n_arr, *refs):
    w_refs, x_refs, sc_ref = refs[:n_arr], refs[n_arr : 2 * n_arr], refs[2 * n_arr]
    packed = half == 1
    out_ref, cnt_ref = refs[-2:]
    k = w_refs[0].shape[1]
    kb = 256
    per = kb // 128
    cols = slice(group * NZ * 128, (group + 1) * NZ * 128)
    for j in range(k // kb):
        rows = slice(j * kb, (j + 1) * kb)
        acc, lanes, pos = None, None, 0
        for a in range(n_arr):
            r = w_refs[a].shape[2]
            sc = sc_ref[half : half + 1, pos : pos + r]
            pos += r
            w = (w_refs[a][half, rows, :].astype(F32) * sc).astype(BF16)
            wf = w.astype(F32)
            for t in range(r // 128):
                part = wf[:, t * 128 : (t + 1) * 128]
                lanes = part if lanes is None else lanes + part
            d = jnp.dot(w, x_refs[a][:, cols], preferred_element_type=F32)
            acc = d if acc is None else acc + d
        col = jnp.sum(lanes.T, axis=0, keepdims=True)
        for t in range(per):
            cnt_ref[j * per + t : j * per + t + 1, :] = col[:, t * 128 : (t + 1) * 128]
        for f in range(NZ):
            out_ref[f, rows, :] = acc[:, f * 128 : (f + 1) * 128].astype(out_ref.dtype)
    if packed:
        for f in range(NZ):
            out_ref[f, k:, :] = _pack_counts(cnt_ref[...])


def _pack_counts(c):
    hi = c.astype(BF16).astype(F32)
    mid = (c - hi).astype(BF16).astype(F32)
    lo = (c - hi) - mid
    return jnp.concatenate([hi, mid, lo, jnp.zeros_like(lo)], axis=0).astype(BF16)


def _unpack_counts(rows):
    t = rows.astype(F32)
    return (t[0:8] + t[8:16]) + t[16:24]


COUNTS = jax.ShapeDtypeStruct((8, 128), F32)


def weighted_sums(half, group, ws, xs, scales, after=()):
    n_arr = len(ws)
    k, r = ws[0].shape[1:]
    operands = [*ws, *xs, scales, *after]
    if half == 1:
        out_shape = jax.ShapeDtypeStruct((NZ, k + COUNT_ROWS, 128), BF16)
        out_specs, scratch = VMEM, [pltpu.VMEM((8, 128), F32)]
    else:
        out_shape = (jax.ShapeDtypeStruct((NZ, k, 128), F32), COUNTS)
        out_specs, scratch = (VMEM, VMEM), []
    return pl.pallas_call(
        functools.partial(_sum_kernel, half, group, n_arr),
        out_shape=out_shape,
        in_specs=[VMEM] * len(operands),
        out_specs=out_specs,
        scratch_shapes=scratch,
        compiler_params=_params(14),
        cost_estimate=COSTS[half],
        name="sums_sib" if half else "sums_own",
    )(*operands)


def _call(kernel, out_shape, args, name, mib=8):
    many = isinstance(out_shape, tuple)
    return pl.pallas_call(
        kernel,
        out_shape=out_shape,
        in_specs=[VMEM] * len(args),
        out_specs=(VMEM,) * len(out_shape) if many else VMEM,
        compiler_params=_params(mib),
        cost_estimate=LIGHT,
        name=name,
    )(*args)


def _mix_kernel(acc_ref, cnt_ref, add_ref, *refs):
    keep_ref, sum_ref = refs[-2:]
    outs = refs[-2 - (NZ - 1) : -2]
    k = acc_ref.shape[1]
    c = cnt_ref[...] + _unpack_counts(add_ref[0, k:, :])
    sum_ref[...] = c
    packed = _pack_counts(c)
    for f in range(NZ - 1):
        outs[f][:k, :] = (acc_ref[f] + add_ref[f, :k, :].astype(F32)).astype(BF16)
        outs[f][k:, :] = packed
    keep_ref[...] = acc_ref[NZ - 1] + add_ref[NZ - 1, :k, :].astype(F32)


def mix(acc, cnt, add):
    k = acc.shape[1]
    out = (jax.ShapeDtypeStruct((k + COUNT_ROWS, 128), BF16),) * (NZ - 1)
    out += (jax.ShapeDtypeStruct((k, 128), F32), COUNTS)
    return _call(_mix_kernel, out, [acc, cnt, add], "mix")


def _totals(keep_ref, cnt_ref, refs):
    k = keep_ref.shape[0]
    total, c = keep_ref[...], cnt_ref[...]
    for r in refs:
        total = total + r[:k, :].astype(F32)
        c = c + _unpack_counts(r[k:, :])
    return total, c


def _far_kernel(keep_ref, cnt_ref, *refs):
    o_ref = refs[-1]
    k = keep_ref.shape[0]
    total, c = _totals(keep_ref, cnt_ref, refs[: NZ - 1])
    o_ref[:k, :] = total.astype(BF16)
    o_ref[k:, :] = _pack_counts(c)


def _final_kernel(id_ref, keep_ref, cnt_ref, *refs):
    other_ref, c_ref, o_ref = refs[-3:]
    k = c_ref.shape[0] // 2
    xh = _dp(id_ref) // NZ
    cols = pl.ds(pl.multiple_of(_dp(id_ref) * 128, 128), 128)
    mine = _totals(keep_ref, cnt_ref, refs[:-3])
    other = other_ref[:k, :].astype(F32), _unpack_counts(other_ref[k:, :])
    for side, (total, c) in ((xh, mine), (1 - xh, other)):
        off = pl.multiple_of(side * k, k)
        cnt = jnp.concatenate([c[q : q + 1, :] for q in range(k // 128)], axis=1)
        top = total + PRIOR * c_ref[pl.ds(off, k), cols].astype(F32)
        o_ref[:, pl.ds(off, k)] = top.T / (cnt + PRIOR)


def finish(ident, parts, other, centroids):
    return pl.pallas_call(
        _final_kernel,
        out_shape=jax.ShapeDtypeStruct((128, centroids.shape[0]), F32),
        in_specs=[SMEM] + [VMEM] * (len(parts) + 2),
        out_specs=VMEM,
        compiler_params=_params(12),
        name="finish",
    )(ident, *parts, other, centroids)


def _slots():
    place = {}
    for a in range(4):
        place[0, a] = (0, a * 128)
        place[2, a] = (3 + a // 2, (a % 2) * 128)
        place[1, a] = (1 if a < 2 else 2, (a % 2) * 128)
        place[3, a] = (1 if a >= 2 else 2, 256 + (a % 2) * 128)
    return [place[b, a] for b in range(4) for a in range(4)]


def _gather_slots(refs, row):
    return jnp.concatenate(
        [refs[n][row : row + 1, off : off + 128] for n, off in _slots()], axis=0
    )


def _merge(pairs, gain):
    m = functools.reduce(jnp.maximum, [p[0] for p in pairs])
    s = sum(p[1] * jnp.exp2(p[0] - m) for p in pairs)
    return m, s


def _absolute(id_ref):
    dp, cent = _dp(id_ref), id_ref[0] % 16
    x, y, core = (dp // NZ) * 2 + cent // 8, (cent // 2) % NY, cent % 2
    first = jnp.where(core == 0, y, x)
    second = jnp.where(core == 0, x, y)
    return [((second - b) % 4) * 4 + (first - a) % 4 for b in range(4) for a in range(4)]


def _pack_kernel(gain, id_ref, *refs):
    stats, o_ref, t_ref = refs[:-2], refs[-2], refs[-1]
    pairs = [(_gather_slots(stats, 2 * b), _gather_slots(stats, 2 * b + 1)) for b in range(2)]
    m, s = _merge(pairs, gain)
    for i, n in enumerate(_absolute(id_ref)):
        t_ref[0, pl.ds(n, 1), :] = m[i : i + 1, :]
        t_ref[1, pl.ds(n, 1), :] = s[i : i + 1, :]
    v = t_ref[...]
    for j in range(o_ref.shape[0]):
        o_ref[j] = v


def _scale_kernel(gain, id_ref, all_ref, *refs):
    stats, o_ref, t_ref = refs[:-2], refs[-2], refs[-1]
    top, total = _merge([(all_ref[j, 0], all_ref[j, 1]) for j in range(all_ref.shape[0])], gain)
    t_ref[0], t_ref[1] = top, total
    order = _absolute(id_ref)
    top, total = [
        jnp.concatenate([t_ref[q, pl.ds(n, 1), :] for n in order], axis=0) for q in range(2)
    ]
    base = [sum(st.shape[1] for st in stats[:n]) for n in range(len(stats))]
    for b in range(2):
        q = jnp.exp2(_gather_slots(stats, 2 * b) - top) / total
        for i, (n, off) in enumerate(_slots()):
            lane = base[n] + off
            o_ref[b : b + 1, lane : lane + 128] = q[i : i + 1, :]


def _statistics(kernel, shape, ident, args, name):
    return pl.pallas_call(
        kernel,
        out_shape=jax.ShapeDtypeStruct(shape, F32),
        in_specs=[SMEM] + [VMEM] * len(args),
        out_specs=VMEM,
        scratch_shapes=[pltpu.VMEM((2, 16, 128), F32)],
        compiler_params=_params(2),
        cost_estimate=LIGHT,
        name=name,
    )(ident, *args)


def _plane_groups():
    return [
        [(xh * 4 + z) * 16 + (xl * 4 + y) * 2 + core
         for xh in range(2) for xl in range(2) for y in range(NY)]
        for z in range(NZ) for core in range(2)
    ]


def local(points, centroids):
    features = points.shape[1]
    gain = BETA_GAIN * features ** (-0.5) * math.log2(math.e)
    ident = lax.axis_index(AXES).astype(jnp.int32).reshape(1)

    shards = [points] + [send_first(points, d) for d in (1, 2, 3)]
    shard, ident = lax.optimization_barrier((centroids, ident))
    whole = (centroids, send_core(shard))
    own, own_norm = load_half(ident, whole[0], 4, gain)
    line_a, line_b = join(shards[0], shards[1], own_norm), join(shards[2], shards[3], own_norm)
    half = line_a.shape[0]
    up_a, down_b = send_second(line_a, 1), send_second(line_b, 3)
    sib, sib_norm = load_half(ident, whole[1], 4, gain)
    cents = (own, sib)
    norms = (own_norm, sib_norm)
    up_b, down_a = send_second(line_b, 1), send_second(line_a, 3)

    ws, stats, xs = [], [], []

    def run(*xin):
        w, st, xp = score(ident, xin, cents, norms, gain, stats[-1:])
        ws.append(w)
        stats.append(st)
        xs.append(xp)

    run(line_a, line_b)
    up_a, down_b, stats[0] = lax.optimization_barrier((up_a, down_b, stats[0]))
    far_b, far_a = send_second(down_b, 3), send_second(up_a, 1)
    run(up_a, down_b)
    run(up_b, down_a)
    run(far_a)
    run(far_b)

    shape = (NX * NY, 2, 16, 128)
    packs = _statistics(functools.partial(_pack_kernel, gain), shape, ident, stats, "stats_pack")
    packs = lax.all_to_all(packs, AXES, 0, 0, tiled=True, axis_index_groups=_plane_groups())
    shape = (8, sum(st.shape[1] for st in stats))
    scales = _statistics(
        functools.partial(_scale_kernel, gain), shape, ident, [packs] + stats, "stats_scale"
    )

    got, order = [], []
    for g in range(2):
        part = send_core(weighted_sums(1, g, ws, xs, scales, order))
        acc, cnt = weighted_sums(0, g, ws, xs, scales, order)
        *blocks, keep, cnt = mix(acc, cnt, part)
        order = [cnt]
        got.append([keep, cnt] + [send_z(v, d) for v, d in zip(blocks, SHIFTS)])
    rows = jax.ShapeDtypeStruct(blocks[0].shape, BF16)
    other = send_far(_call(_far_kernel, rows, got[0] + order, "far_sum"))
    return finish(ident, got[1], other, centroids)


def solution(mesh):
    return jax.shard_map(
        local,
        mesh=mesh,
        in_specs=(P(("dp", "cent"), None), P("cent", None)),
        out_specs=P("dp", "cent"),
        check_vma=False,
    )
```
